256 devices in a mesh: dp: 32 (over z, y), chan: 8 (over x, core).
Axes of the slice: x: 4, y: 4, z: 8, core: 2. Of those that a mesh axis runs over, the one named last changes fastest.
Arguments:
- inputs: bfloat16 [12544, 2048], P('dp', 'chan'), may hold values from -6 to 6
- conv_one: bfloat16 [9, 32, 2048], P(None, None, 'chan'), may hold values from -0.375 to 0.375
- conv_two: bfloat16 [9, 32, 2048], P(None, None, 'chan'), may hold values from -0.375 to 0.375
- probe_one: bfloat16 [2048, 512], P('chan'), may hold values from -0.125 to 0.125
- probe_two: bfloat16 [2048, 512], P('chan'), may hold values from -0.125 to 0.125
Outputs:
- restored: bfloat16 [12544, 2048], P('dp', 'chan')
- triangle: float32 [512, 512], replicated
The draws below stay inside these ranges and needn't reach their ends.
All inputs are finite; a program needn't handle non-finite values.
Results may differ from the reference program's by a relative error of at most 0.028.
Values may be sent and summed in bfloat16 or wider, within the bound.
No kernel may reach another device: no remote copies, remote signals or barrier semaphores. Data moves between devices by JAX's collectives and lax.ppermute only.
A program may use at most 64 MiB of HBM per device.

```python
import math
import jax
import jax.numpy as jnp
from jax import lax

C = 2048
GROUP = 32
K = 512
SIDE = 7
ROWS = 12544


def shard_levels(rng, dims, cuts, low, top_value):
    loudness = 1.0
    for dim, blocks in cuts:
        steps = jax.random.uniform(jax.random.fold_in(jax.random.fold_in(rng, 6), dim), (blocks,), jnp.float32, low / len(cuts), top_value / len(cuts))
        loudness = loudness * jnp.repeat(jnp.exp(steps), dims[dim] // blocks).reshape((-1,) + (1,) * (len(dims) - 1 - dim))
    return loudness


def scatter_about(rng, dims, width, bound, cuts=(), dtype=jnp.bfloat16):
    factor_of = shard_levels(rng, dims, cuts, -0.22, 0.18) if cuts else 1.0
    drawn = jax.random.normal(rng, dims, jnp.float32) * width * factor_of
    return jnp.minimum(jnp.maximum(drawn, -bound), bound).astype(dtype)


def setup_inputs(seed: int = 0) -> dict:
    seeds = jax.random.split(jax.random.key(seed), 6)
    return {
        "inputs": scatter_about(seeds[0], (ROWS, C), 1.0, 6.0, ((0, 32), (1, 8))),
        "conv_one": scatter_about(seeds[1], (9, GROUP, C), (9 * GROUP) ** -0.5, 0.375, ((2, 8),)),
        "conv_two": scatter_about(seeds[2], (9, GROUP, C), (9 * GROUP) ** -0.5, 0.375, ((2, 8),)),
        "probe_one": scatter_about(seeds[3], (C, K), C ** -0.5, 0.125, ((0, 8),)),
        "probe_two": scatter_about(seeds[4], (C, K), C ** -0.5, 0.125, ((0, 8),)),
    }


def convolve(field, weight):
    total_rows = field.shape[0]
    group_width = weight.shape[1]
    groups = C // group_width
    images = field.reshape(total_rows // (SIDE * SIDE), SIDE, SIDE, C)
    padded = jnp.pad(images, ((0, 0), (1, 1), (1, 1), (0, 0)))
    total = jnp.zeros((total_rows, groups, group_width), jnp.float32)
    for offset in range(9):
        row_shift = offset // 3
        col_shift = offset % 3
        window = padded[:, row_shift:row_shift + SIDE, col_shift:col_shift + SIDE, :]
        window = window.reshape(total_rows, groups, group_width).astype(jnp.float32)
        kernel = weight[offset].reshape(group_width, groups, group_width).astype(jnp.float32)
        total = total + jnp.einsum('pgi,igo->pgo', window, kernel)
    return total.reshape(total_rows, C).astype(jnp.bfloat16)

def compress(responses, probe):
    sketch = jnp.dot(responses.astype(jnp.float32), probe.astype(jnp.float32), preferred_element_type=jnp.float32).astype(jnp.bfloat16)
    gram = lax.dot_general(sketch.astype(jnp.float32), sketch.astype(jnp.float32), (((0,), (0,)), ((), ())), preferred_element_type=jnp.float32)
    cross = lax.dot_general(sketch.astype(jnp.float32), responses.astype(jnp.float32), (((0,), (0,)), ((), ())), preferred_element_type=jnp.float32)
    lower = jnp.linalg.cholesky(gram)
    coeffs = lax.linalg.triangular_solve(lower, cross, left_side=True, lower=True).astype(jnp.bfloat16)
    mapped = lax.linalg.triangular_solve(lower, coeffs.astype(jnp.float32), left_side=True, lower=True, transpose_a=True).astype(jnp.bfloat16)
    return (jnp.dot(sketch.astype(jnp.float32), mapped.astype(jnp.float32), preferred_element_type=jnp.float32).astype(jnp.bfloat16), lower)

def reference(inputs, conv_one, conv_two, probe_one, probe_two):
    responses_one = convolve(inputs, conv_one)
    restored_one, lower_one = compress(responses_one, probe_one)
    activated = jnp.maximum(restored_one, jnp.zeros((), jnp.bfloat16))
    responses_two = convolve(activated, conv_two)
    restored, lower_two = compress(responses_two, probe_two)
    triangle = jnp.transpose(lower_two) * (1.0 / math.sqrt(ROWS))
    return (restored, triangle)
```

```python
import functools
import math

import jax
import jax.numpy as jnp
from jax import lax
from jax.experimental import pallas as pl
from jax.experimental.pallas import tpu as pltpu
from jax.sharding import Mesh, PartitionSpec as P

SIDE = 7
K = 512
NB = 128
HALF = 256
F32 = jnp.float32
BF16 = jnp.bfloat16
HI = lax.Precision.HIGHEST
VMEM = pl.BlockSpec(memory_space=pltpu.VMEM)
SMEM = pl.BlockSpec(memory_space=pltpu.SMEM)
PARAMS = pltpu.CompilerParams(vmem_limit_bytes=48 << 20)
BLOCKS = (((0, 0), (0, 1), (0, 2), (0, 3), (1, 1)), ((1, 2), (1, 3), (2, 2), (2, 3), (3, 3)))
NG = 5 * NB


def dot(a, b, dims=((1,), (0,)), precision=None):
    return lax.dot_general(
        a, b, (dims, ((), ())), precision=precision, preferred_element_type=F32
    )


def bcast_lane(x, k):
    return jnp.broadcast_to(x[:, k : k + 1], (8, NB))


def bcast_row(x, k):
    return jnp.broadcast_to(x[k : k + 1, :], (8, NB))


def factor(rows):
    n = len(rows)
    sub = lax.broadcasted_iota(jnp.int32, (8, NB), 0)
    lane = lax.broadcasted_iota(jnp.int32, (8, NB), 1)
    inv = [(lane == sub + 8 * r).astype(F32) for r in range(n)]
    rows = list(rows)
    upper, lower_inv = [], []
    for r in range(n):
        top, top_inv = rows[r], inv[r]
        cols = [bcast_lane(top, 8 * r + k) for k in range(8)]
        s = {(i, k): bcast_row(cols[k], i) for k in range(8) for i in range(k, 8)}
        m, d = {}, []
        for k in range(8):
            d.append(s[k, k])
            over = 1.0 / s[k, k]
            for i in range(k + 1, 8):
                m[i, k] = s[i, k] * over
            for j in range(k + 1, 8):
                for i in range(j, 8):
                    s[i, j] = s[i, j] - m[i, k] * s[j, k]
        t = {}
        for j in range(8):
            for i in range(j + 1, 8):
                v = m[i, j]
                for k in range(j + 1, i):
                    v = v + m[i, k] * t[k, j]
                t[i, j] = -v
        q = [lax.rsqrt(x) for x in d]
        u = v = None
        for j in range(8):
            c = jnp.where(sub == j, q[j], 0.0)
            for i in range(j + 1, 8):
                c = jnp.where(sub == i, q[i] * t[i, j], c)
            uj, vj = c * bcast_row(top, j), c * bcast_row(top_inv, j)
            u, v = (uj, vj) if u is None else (u + uj, v + vj)
        upper.append(jnp.where(lane >= 8 * r + sub, u, 0.0))
        lower_inv.append(v)
        ub = [bcast_row(u, k) for k in range(8)]
        vb = [bcast_row(v, k) for k in range(8)]
        for g in range(r + 1, n):
            cg = [bcast_lane(rows[g], 8 * r + k) for k in range(8)]
            a, w = rows[g], inv[g]
            for k in range(8):
                l = cg[k]
                for j in range(k):
                    l = l + t[k, j] * cg[j]
                l = q[k] * l
                a, w = a - l * ub[k], w - l * vb[k]
            rows[g], inv[g] = a, w
    return upper, lower_inv


def solve_body(core, pack_ref, other_ref, lt_ref, a_ref, v_ref, g_ref):
    mine = pl.multiple_of(core * NG, NG)
    theirs = pl.multiple_of((1 - core) * NG, NG)
    g_ref[pl.ds(mine, NG), :] = pack_ref[:NG, :]
    g_ref[pl.ds(theirs, NG), :] = other_ref[...]
    for c in range(2):
        for n, (i, j) in enumerate(BLOCKS[c]):
            p = (5 * c + n) * NB
            a_ref[i * NB : (i + 1) * NB, j * NB : (j + 1) * NB] = g_ref[p : p + NB, :]
    for h in range(2):
        p = NG + h * K
        a_ref[:, K + h * NB : K + (h + 1) * NB] = pack_ref[p : p + K, :]
    lt_ref[...] = jnp.zeros(lt_ref.shape, F32)
    for b in range(4):
        o = b * NB
        u, v = factor([a_ref[o + 8 * i : o + 8 * i + 8, o : o + NB] for i in range(16)])
        for i in range(16):
            lt_ref[o + 8 * i : o + 8 * i + 8, o : o + NB] = u[i]
            v_ref[o + 8 * i : o + 8 * i + 8, :] = v[i]
        vb = v_ref[o : o + NB, :]
        if b < 3:
            lt_ref[o : o + NB, o + NB : K] = dot(vb, a_ref[o : o + NB, o + NB : K], precision=HI)
        a_ref[o : o + NB, K:] = dot(vb, a_ref[o : o + NB, K:], precision=HI)
        for r in range(b + 1, 4):
            p = r * NB
            ubr = lt_ref[o : o + NB, p : p + NB]
            a_ref[p : p + NB, p:K] -= dot(ubr, lt_ref[o : o + NB, p:K], ((0,), (0,)), HI)
            a_ref[p : p + NB, K:] -= dot(ubr, a_ref[o : o + NB, K:], ((0,), (0,)), HI)
    xs = [None] * 4
    for b in (3, 2, 1, 0):
        o = b * NB
        y = a_ref[o : o + NB, K:].astype(BF16).astype(F32)
        for c in range(b + 1, 4):
            y = y - dot(lt_ref[o : o + NB, c * NB : (c + 1) * NB], xs[c], precision=HI)
        xs[b] = dot(v_ref[o : o + NB, :], y, ((0,), (0,)), HI)
    return [x.astype(BF16) for x in xs]


def conv_body(core, w_ref, p_ref, r_ref, keep_ref, send_ref, pad_ref, win_ref, bd_ref):
    n = r_ref.shape[0]
    width = r_ref.shape[1]
    group = w_ref.shape[1]
    row = lax.broadcasted_iota(jnp.int32, (n, width), 0)
    q = lax.rem(row, SIDE * SIDE)
    y, x = lax.div(q, SIDE), lax.rem(q, SIDE)
    bi = lax.broadcasted_iota(jnp.int32, (width, width), 0)
    bj = lax.broadcasted_iota(jnp.int32, (width, width), 1)
    same = lax.div(bi, group) == lax.div(bj, group)
    for tap in range(9):
        a, b = tap // 3 - 1, tap % 3 - 1
        d = 8 + a * SIDE + b
        window = pad_ref[d : d + n, :]
        ok = None
        if a:
            ok = (y > 0) if a < 0 else (y < SIDE - 1)
        if b:
            okx = (x > 0) if b < 0 else (x < SIDE - 1)
            ok = okx if ok is None else ok & okx
        if ok is not None:
            window = jnp.where(ok, window, 0.0)
        win_ref[:, tap * width : (tap + 1) * width] = window.astype(BF16)
        tiled = jnp.concatenate([w_ref[tap].astype(F32)] * (width // group), axis=0)
        bd_ref[tap * width : (tap + 1) * width, :] = jnp.where(same, tiled, 0.0).astype(BF16)
    r = dot(win_ref[...], bd_ref[...]).astype(BF16)
    r_ref[...] = r
    mine = pl.multiple_of(core * HALF, HALF)
    theirs = pl.multiple_of((1 - core) * HALF, HALF)
    send_ref[...] = dot(r, p_ref[:, pl.ds(theirs, HALF)]).astype(BF16)
    keep_ref[...] = dot(r, p_ref[:, pl.ds(mine, HALF)])


def pad_field(pad_ref, field):
    n, width = field.shape
    pad_ref[0:8, :] = jnp.zeros((8, width), F32)
    pad_ref[8 + n : 16 + n, :] = jnp.zeros((8, width), F32)
    pad_ref[8 : 8 + n, :] = field


def first_kernel(core_ref, f_ref, w_ref, p_ref, r_ref, keep_ref, send_ref, pad_ref, win_ref, bd_ref):
    pad_field(pad_ref, f_ref[...].astype(F32))
    conv_body(core_ref[0], w_ref, p_ref, r_ref, keep_ref, send_ref, pad_ref, win_ref, bd_ref)


def middle_kernel(core_ref, pack_ref, other_ref, s_ref, w_ref, p_ref, r_ref, keep_ref, send_ref,
                  lt_ref, a_ref, v_ref, g_ref, pad_ref, win_ref, bd_ref):
    core = core_ref[0]
    xs = solve_body(core, pack_ref, other_ref, lt_ref, a_ref, v_ref, g_ref)
    restored = dot(s_ref[...], jnp.concatenate(xs, axis=0)).astype(BF16).astype(F32)
    pad_field(pad_ref, jnp.maximum(restored, 0.0))
    conv_body(core, w_ref, p_ref, r_ref, keep_ref, send_ref, pad_ref, win_ref, bd_ref)


def last_kernel(scale, core_ref, pack_ref, other_ref, s_ref, out_ref, tri_ref,
                lt_ref, a_ref, v_ref, g_ref):
    xs = solve_body(core_ref[0], pack_ref, other_ref, lt_ref, a_ref, v_ref, g_ref)
    tri_ref[...] = lt_ref[...] * scale
    out_ref[...] = dot(s_ref[...], jnp.concatenate(xs, axis=0)).astype(BF16)


def gram_kernel(core_ref, own_ref, other_ref, r_ref, s_ref, m_ref):
    core = core_ref[0]
    s_ref[:, pl.ds(pl.multiple_of(core * HALF, HALF), HALF)] = own_ref[...]
    s_ref[:, pl.ds(pl.multiple_of((1 - core) * HALF, HALF), HALF)] = other_ref[...]
    s = s_ref[...]
    cross = dot(s, r_ref[...], ((0,), (0,)))
    for h in range(2):
        m_ref[NG + h * K : NG + (h + 1) * K, :] = cross[:, h * NB : (h + 1) * NB]
    m_ref[NG + 2 * K :, :] = jnp.zeros((NB, NB), F32)
    for c in range(2):

        @pl.when(core == c)
        def _():
            for n, (i, j) in enumerate(BLOCKS[c]):
                block = dot(
                    s_ref[:, i * NB : (i + 1) * NB], s_ref[:, j * NB : (j + 1) * NB], ((0,), (0,))
                )
                m_ref[n * NB : (n + 1) * NB, :] = block


def solve_scratch():
    return [
        pltpu.VMEM((K, K), F32),
        pltpu.VMEM((K, K + HALF), F32),
        pltpu.VMEM((K, NB), F32),
        pltpu.VMEM((2 * NG, NB), F32),
    ]


def conv_scratch(n, width):
    return [
        pltpu.VMEM((n + 16, width), F32),
        pltpu.VMEM((n, 9 * width), BF16),
        pltpu.VMEM((9 * width, width), BF16),
    ]


def conv_outs(n, width):
    return (
        jax.ShapeDtypeStruct((n, width), BF16),
        jax.ShapeDtypeStruct((n, HALF), F32),
        jax.ShapeDtypeStruct((n, HALF), BF16),
    )


def call(kernel, name, outs, args, scratch=()):
    return pl.pallas_call(
        kernel,
        out_shape=outs,
        in_specs=[SMEM] + [VMEM] * (len(args) - 1),
        out_specs=jax.tree.map(lambda _: VMEM, outs),
        scratch_shapes=list(scratch),
        compiler_params=PARAMS,
        name=name,
    )(*args)


SWAP = ((0, 1), (1, 0))


def spread(x, axes):
    n = lax.axis_size(axes)
    return lax.all_to_all(jnp.broadcast_to(x[None], (n,) + x.shape), axes, 0, 0)


def sketch_of(keep, send):
    pair = (keep + lax.ppermute(send, "core", SWAP).astype(F32)).astype(BF16)
    own = jnp.sum(spread(pair, "x").astype(F32), axis=0).astype(BF16)
    return own, lax.ppermute(own, "core", SWAP)


def reduce_pack(m):
    n = lax.axis_size(("z", "y"))
    parts = lax.all_to_all(m.reshape(n, m.shape[0] // n, NB), ("z", "y"), 0, 0)
    pack = spread(jnp.sum(parts, axis=0), ("z", "y")).reshape(m.shape)
    return pack, lax.ppermute(pack[:NG], "core", SWAP)


def compress_sums(core, r, keep, send):
    own, other = sketch_of(keep, send)
    n = r.shape[0]
    outs = (
        jax.ShapeDtypeStruct((n, K), BF16),
        jax.ShapeDtypeStruct((NG + 2 * K + NB, NB), F32),
    )
    s, m = call(gram_kernel, "gram", outs, (core, own, other, r))
    pack, gram_other = reduce_pack(m)
    return pack, gram_other, s


def per_device(inputs, conv_one, conv_two, probe_one, probe_two):
    n, width = inputs.shape
    total_rows = n * lax.axis_size(("z", "y"))
    core = lax.axis_index("core").astype(jnp.int32).reshape(1)
    outs = conv_outs(n, width)
    r, keep, send = call(
        first_kernel, "first", outs, (core, inputs, conv_one, probe_one), conv_scratch(n, width)
    )
    sums = compress_sums(core, r, keep, send)
    r, keep, send = call(
        middle_kernel, "middle", outs, (core, *sums, conv_two, probe_two),
        solve_scratch() + conv_scratch(n, width),
    )
    sums = compress_sums(core, r, keep, send)
    outs = (jax.ShapeDtypeStruct((n, width), BF16), jax.ShapeDtypeStruct((K, K), F32))
    return call(
        functools.partial(last_kernel, 1.0 / math.sqrt(total_rows)), "last", outs, (core, *sums),
        solve_scratch(),
    )


def solution(mesh):
    grid = Mesh(mesh.devices.reshape(8, 4, 4, 2), ("z", "y", "x", "core"))
    rows, chan = ("z", "y"), ("x", "core")
    in_specs = (
        P(rows, chan),
        P(None, None, chan),
        P(None, None, chan),
        P(chan, None),
        P(chan, None),
    )
    out_specs = (P(rows, chan), P())
    return jax.shard_map(
        per_device, mesh=grid, in_specs=in_specs, out_specs=out_specs, check_vma=False
    )
```

```python
import functools
import math

import jax
import jax.numpy as jnp
from jax import lax
from jax.experimental import pallas as pl
from jax.experimental.pallas import tpu as pltpu
from jax.sharding import Mesh, PartitionSpec as P

SIDE = 7
K = 512
NB = 128
HALF = 256
F32 = jnp.float32
BF16 = jnp.bfloat16
HI = lax.Precision.HIGHEST
VMEM = pl.BlockSpec(memory_space=pltpu.VMEM)
SMEM = pl.BlockSpec(memory_space=pltpu.SMEM)
PARAMS = pltpu.CompilerParams(vmem_limit_bytes=48 << 20)
BLOCKS = (((0, 0), (0, 1), (0, 2), (0, 3), (1, 1)), ((1, 2), (1, 3), (2, 2), (2, 3), (3, 3)))
NG = 5 * NB


def dot(a, b, dims=((1,), (0,)), precision=None):
    return lax.dot_general(
        a, b, (dims, ((), ())), precision=precision, preferred_element_type=F32
    )


def bcast_lane(x, k):
    return jnp.broadcast_to(x[:, k : k + 1], (8, NB))


def bcast_row(x, k):
    return jnp.broadcast_to(x[k : k + 1, :], (8, NB))


def combine(coeffs, rows):
    p = [c * b for c, b in zip(coeffs, rows)]
    while len(p) > 1:
        p = [p[i] + p[i + 1] for i in range(0, len(p), 2)]
    return p[0]


def factor(rows):
    n = len(rows)
    sub = lax.broadcasted_iota(jnp.int32, (8, NB), 0)
    lane = lax.broadcasted_iota(jnp.int32, (8, NB), 1)
    at = [sub == i for i in range(8)]
    inv = [(lane == sub + 8 * r).astype(F32) for r in range(n)]
    rows = list(rows)
    upper, lower_inv = [], []
    zero = jnp.zeros((8, NB), F32)
    for r in range(n):
        top, top_inv = rows[r], inv[r]
        cols = [bcast_lane(top, 8 * r + k) for k in range(8)]
        s = {(i, k): bcast_row(cols[k], i) for k in range(8) for i in range(k, 8)}
        m, d = {}, [None] * 8
        for k in range(0, 8, 2):
            a, b, c = s[k, k], s[k + 1, k], s[k + 1, k + 1]
            det = a * c - b * b
            both = 1.0 / (a * det)
            ia, idet = both * det, both * a
            m[k + 1, k] = b * ia
            d[k], d[k + 1] = a, det * ia
            n0 = {i: s[i, k] * c - s[i, k + 1] * b for i in range(k + 2, 8)}
            n1 = {i: s[i, k + 1] * a - s[i, k] * b for i in range(k + 2, 8)}
            for j in range(k + 2, 8):
                for i in range(j, 8):
                    s[i, j] = s[i, j] - (n0[i] * s[j, k] + n1[i] * s[j, k + 1]) * idet
            for i in range(k + 2, 8):
                m[i, k], m[i, k + 1] = s[i, k] * ia, n1[i] * idet
        t = {}
        for j in range(8):
            for i in range(j + 1, 8):
                v = m[i, j]
                for k in range(j + 1, i):
                    v = v + m[i, k] * t[k, j]
                t[i, j] = -v
        q = [lax.rsqrt(x) for x in d]
        t = {(i, j): q[i] * t[i, j] if i > j else q[i] for j in range(8) for i in range(j, 8)}
        by_col, by_row = [], []
        for j in range(8):
            c = zero
            for i in range(j, 8):
                c = jnp.where(at[i], t[i, j], c)
            by_col.append(c)
            c = zero
            for i in range(j + 1):
                c = jnp.where(at[i], t[j, i], c)
            by_row.append(c)
        rb = [bcast_row(top, j) for j in range(8)]
        ib = [bcast_row(top_inv, j) for j in range(8)]
        upper.append(jnp.where(lane >= 8 * r + sub, combine(by_col, rb), 0.0))
        lower_inv.append(combine(by_col, ib))
        if r == n - 1:
            break
        block = []
        for j in range(8):
            c = by_row[j] * t[j, j]
            for i in range(j + 1, 8):
                c = c + by_row[i] * t[i, j]
            block.append(c)
        x, xi = combine(block, rb), combine(block, ib)
        xb = [bcast_row(x, k) for k in range(8)]
        xib = [bcast_row(xi, k) for k in range(8)]
        for g in range(r + 1, n):
            cg = [bcast_lane(rows[g], 8 * r + k) for k in range(8)]
            rows[g], inv[g] = rows[g] - combine(cg, xb), inv[g] - combine(cg, xib)
    return upper, lower_inv


def unpack(pack_ref, t_ref, g_ref, base):
    t_ref[...] = pack_ref[...].astype(F32)
    part = NG // t_ref.shape[0]
    for i in range(t_ref.shape[0]):
        g_ref[pl.ds(base + i * part, part), :] = t_ref[i, :part, :] + t_ref[i, part : 2 * part, :]


def solve_body(core, pack_ref, other_ref, corr_ref, lt_ref, a_ref, v_ref, g_ref, t_ref):
    unpack(other_ref, t_ref, g_ref, (1 - core) * NG)
    unpack(pack_ref, t_ref, g_ref, core * NG)
    pieces = t_ref.shape[0]
    part = 2 * NG // pieces
    for i in range(pieces):
        h, o = divmod(i * (2 * K // pieces), K)
        rows = slice(o, o + 2 * K // pieces)
        lanes = slice(h * NB, (h + 1) * NB)
        a_ref[rows, K + h * NB : K + (h + 1) * NB] = t_ref[i, part:, :] + corr_ref[rows, lanes]
    blocks = {}
    for c in range(2):
        for n, ij in enumerate(BLOCKS[c]):
            blocks[ij] = (5 * c + n) * NB
    diag = lax.broadcasted_iota(jnp.int32, (NB, NB), 0) == lax.broadcasted_iota(
        jnp.int32, (NB, NB), 1
    )
    drow, qrow, qcol = [], [], []
    for b in range(4):
        p = blocks[b, b]
        only = jnp.where(diag, g_ref[p : p + NB, :], 0.0)
        drow.append(jnp.sum(only, axis=0, keepdims=True))
        qrow.append(lax.rsqrt(drow[b]))
        qcol.append(lax.rsqrt(jnp.sum(only, axis=1, keepdims=True)))
    for (i, j), p in blocks.items():
        a_ref[i * NB : (i + 1) * NB, j * NB : (j + 1) * NB] = (
            g_ref[p : p + NB, :] * qcol[i] * qrow[j]
        )
    for b in range(4):
        a_ref[b * NB : (b + 1) * NB, K:] *= qcol[b]
    lt_ref[...] = jnp.zeros(lt_ref.shape, F32)
    for b in range(4):
        o = b * NB
        u, v = factor([a_ref[o + 8 * i : o + 8 * i + 8, o : o + NB] for i in range(16)])
        for i in range(16):
            lt_ref[o + 8 * i : o + 8 * i + 8, o : o + NB] = u[i]
            v_ref[o + 8 * i : o + 8 * i + 8, :] = v[i]
        vb = v_ref[o : o + NB, :]
        for c in range(b + 1, 4):
            p = c * NB
            ubc = dot(vb, a_ref[o : o + NB, p : p + NB], precision=HI)
            lt_ref[o : o + NB, p : p + NB] = ubc
            if c == b + 1:
                a_ref[p : p + NB, p : p + NB] -= dot(ubc, ubc, ((0,), (0,)), HI)
        a_ref[o : o + NB, K:] = dot(vb, a_ref[o : o + NB, K:], precision=HI)
        for r in range(b + 1, 4):
            p = r * NB
            ubr = lt_ref[o : o + NB, p : p + NB]
            e = p + NB if r == b + 1 else p
            if e < K:
                a_ref[p : p + NB, e:K] -= dot(ubr, lt_ref[o : o + NB, e:K], ((0,), (0,)), HI)
            a_ref[p : p + NB, K:] -= dot(ubr, a_ref[o : o + NB, K:], ((0,), (0,)), HI)
    xs = [None] * 4
    for b in (3, 2, 1, 0):
        o = b * NB
        y = a_ref[o : o + NB, K:].astype(BF16).astype(F32)
        for c in range(b + 1, 4):
            y = y - dot(lt_ref[o : o + NB, c * NB : (c + 1) * NB], xs[c], precision=HI)
        xs[b] = dot(v_ref[o : o + NB, :], y, ((0,), (0,)), HI)
    return [(x * q).astype(BF16) for x, q in zip(xs, qcol)], [d * q for d, q in zip(drow, qrow)]


def conv_body(core, w_ref, p_ref, r_ref, keep_ref, send_ref, pad_ref, win_ref, bd_ref):
    n = r_ref.shape[0]
    width = r_ref.shape[1]
    group = w_ref.shape[1]
    row = lax.broadcasted_iota(jnp.int32, (n, width), 0)
    q = lax.rem(row, SIDE * SIDE)
    y, x = lax.div(q, SIDE), lax.rem(q, SIDE)
    bi = lax.broadcasted_iota(jnp.int32, (width, width), 0)
    bj = lax.broadcasted_iota(jnp.int32, (width, width), 1)
    same = lax.div(bi, group) == lax.div(bj, group)
    for tap in range(9):
        a, b = tap // 3 - 1, tap % 3 - 1
        d = 8 + a * SIDE + b
        window = pad_ref[d : d + n, :]
        ok = None
        if a:
            ok = (y > 0) if a < 0 else (y < SIDE - 1)
        if b:
            okx = (x > 0) if b < 0 else (x < SIDE - 1)
            ok = okx if ok is None else ok & okx
        if ok is not None:
            window = jnp.where(ok, window, 0.0)
        win_ref[:, tap * width : (tap + 1) * width] = window.astype(BF16)
        tiled = jnp.concatenate([w_ref[tap].astype(F32)] * (width // group), axis=0)
        bd_ref[tap * width : (tap + 1) * width, :] = jnp.where(same, tiled, 0.0).astype(BF16)
    r = dot(win_ref[...], bd_ref[...]).astype(BF16)
    r_ref[...] = r
    mine = pl.multiple_of(core * HALF, HALF)
    theirs = pl.multiple_of((1 - core) * HALF, HALF)
    send_ref[...] = dot(r, p_ref[:, pl.ds(theirs, HALF)]).astype(BF16)
    keep_ref[...] = dot(r, p_ref[:, pl.ds(mine, HALF)])


def pad_field(pad_ref, field):
    n, width = field.shape
    pad_ref[0:8, :] = jnp.zeros((8, width), F32)
    pad_ref[8 + n : 16 + n, :] = jnp.zeros((8, width), F32)
    pad_ref[8 : 8 + n, :] = field


def first_kernel(core_ref, f_ref, w_ref, p_ref, r_ref, keep_ref, send_ref, pad_ref, win_ref, bd_ref):
    pad_field(pad_ref, f_ref[...].astype(F32))
    conv_body(core_ref[0], w_ref, p_ref, r_ref, keep_ref, send_ref, pad_ref, win_ref, bd_ref)


def middle_kernel(core_ref, pack_ref, other_ref, corr_ref, s_ref, w_ref, p_ref, r_ref, keep_ref,
                  send_ref, lt_ref, a_ref, v_ref, g_ref, t_ref, pad_ref, win_ref, bd_ref):
    core = core_ref[0]
    xs, _ = solve_body(
        core, pack_ref, other_ref, corr_ref, lt_ref, a_ref, v_ref, g_ref, t_ref
    )
    restored = dot(s_ref[...], jnp.concatenate(xs, axis=0)).astype(BF16).astype(F32)
    pad_field(pad_ref, jnp.maximum(restored, 0.0))
    conv_body(core, w_ref, p_ref, r_ref, keep_ref, send_ref, pad_ref, win_ref, bd_ref)


def last_kernel(scale, core_ref, pack_ref, other_ref, corr_ref, s_ref, out_ref, tri_ref,
                lt_ref, a_ref, v_ref, g_ref, t_ref):
    xs, roots = solve_body(
        core_ref[0], pack_ref, other_ref, corr_ref, lt_ref, a_ref, v_ref, g_ref, t_ref
    )
    for b, root in enumerate(roots):
        lanes = slice(b * NB, (b + 1) * NB)
        tri_ref[:, lanes] = lt_ref[:, lanes] * (root * scale)
    out_ref[...] = dot(s_ref[...], jnp.concatenate(xs, axis=0)).astype(BF16)


def gram_kernel(core_ref, own_ref, other_ref, r_ref, s_ref, m_ref, g_ref, t_ref):
    core = core_ref[0]
    n = own_ref.shape[0]
    pieces = t_ref.shape[0]
    s_ref[:, pl.ds(pl.multiple_of(core * HALF, HALF), HALF)] = own_ref[...]
    s_ref[:, pl.ds(pl.multiple_of((1 - core) * HALF, HALF), HALF)] = other_ref[...]
    s, r = s_ref[...], r_ref[...]
    ones = jnp.ones((8, n), BF16)
    mean = (dot(ones, s) * (1.0 / n)).astype(BF16).astype(F32)
    total = dot(ones, r)
    high = total.astype(BF16).astype(F32)
    low = (total - high).astype(BF16).astype(F32)
    first = lax.broadcasted_iota(jnp.int32, (8, K), 0) < 1
    left = jnp.where(lax.broadcasted_iota(jnp.int32, (8, K), 0) < 2, mean, 0.0).astype(BF16)
    right = jnp.where(first[:, :HALF], high, low).astype(BF16)
    cross = dot(s, r, ((0,), (0,))) - dot(left, right, ((0,), (0,)))
    extra = jnp.concatenate(
        [mean[:1, h * NB : (h + 1) * NB] for h in range(4)]
        + [high[:1, h * NB : (h + 1) * NB] for h in range(2)]
        + [low[:1, h * NB : (h + 1) * NB] for h in range(2)],
        axis=0,
    )
    for c in range(2):

        @pl.when(core == c)
        def _():
            for k, (i, j) in enumerate(BLOCKS[c]):
                block = dot(
                    s_ref[:, i * NB : (i + 1) * NB], s_ref[:, j * NB : (j + 1) * NB], ((0,), (0,))
                )
                g_ref[k * NB : (k + 1) * NB, :] = block

    part = NG // pieces
    step = 2 * K // pieces
    for i in range(pieces):
        g = g_ref[i * part : (i + 1) * part, :]
        hi = g.astype(BF16).astype(F32)
        t_ref[i, :part, :] = hi
        t_ref[i, part : 2 * part, :] = g - hi
        h, o = divmod(i * step, K)
        t_ref[i, 2 * part : 2 * part + step, :] = cross[o : o + step, h * NB : (h + 1) * NB]
        t_ref[i, 2 * part + step :, :] = extra
    m_ref[...] = t_ref[...].astype(BF16)


def sum_kernel(core_ref, parts_ref, out_ref, corr_ref, left_ref, right_ref):
    pieces, rows = parts_ref.shape[:2]
    part = NG // pieces
    keep = rows - 8
    acc = parts_ref[0, :keep, :].astype(F32)
    for i in range(1, pieces):
        acc = acc + parts_ref[i, :keep, :].astype(F32)
    g = acc[:part] + acc[part : 2 * part]
    hi = g.astype(BF16).astype(F32)
    total = jnp.concatenate([hi, g - hi, acc[2 * part :]], axis=0).astype(BF16)
    for i in range(pieces):
        out_ref[i] = total
    for i in range(pieces):
        e = parts_ref[i, keep:, :].astype(F32)
        for h in range(4):
            for k in range(2):
                left_ref[pieces * k + i : pieces * k + i + 1, h * NB : (h + 1) * NB] = e[h : h + 1]
        for h in range(2):
            for k in range(2):
                right_ref[pieces * k + i : pieces * k + i + 1, h * NB : (h + 1) * NB] = e[
                    4 + 2 * k + h : 5 + 2 * k + h
                ]
    corr_ref[...] = dot(left_ref[...].astype(BF16), right_ref[...].astype(BF16), ((0,), (0,)))


def fold_kernel(core_ref, parts_ref, out_ref):
    acc = parts_ref[0].astype(F32)
    for i in range(1, parts_ref.shape[0]):
        acc = acc + parts_ref[i].astype(F32)
    out_ref[...] = acc.astype(BF16)


def solve_scratch(pieces):
    return [
        pltpu.VMEM((K, K), F32),
        pltpu.VMEM((K, K + HALF), F32),
        pltpu.VMEM((K, NB), F32),
        pltpu.VMEM((2 * NG, NB), F32),
        pltpu.VMEM((pieces, 2 * (NG + K) // pieces, NB), F32),
    ]


def conv_scratch(n, width):
    return [
        pltpu.VMEM((n + 16, width), F32),
        pltpu.VMEM((n, 9 * width), BF16),
        pltpu.VMEM((9 * width, width), BF16),
    ]


def conv_outs(n, width):
    return (
        jax.ShapeDtypeStruct((n, width), BF16),
        jax.ShapeDtypeStruct((n, HALF), F32),
        jax.ShapeDtypeStruct((n, HALF), BF16),
    )


def call(kernel, name, outs, args, scratch=()):
    return pl.pallas_call(
        kernel,
        out_shape=outs,
        in_specs=[SMEM] + [VMEM] * (len(args) - 1),
        out_specs=jax.tree.map(lambda _: VMEM, outs),
        scratch_shapes=list(scratch),
        compiler_params=PARAMS,
        name=name,
    )(*args)


SWAP = ((0, 1), (1, 0))
ROWS = ("z", "y")


def spread(x, axes):
    n = lax.axis_size(axes)
    return lax.all_to_all(jnp.broadcast_to(x[None], (n,) + x.shape), axes, 0, 0)


def sketch_of(core, keep, send):
    pair = (keep + lax.ppermute(send, "core", SWAP).astype(F32)).astype(BF16)
    own = call(
        fold_kernel, "fold", jax.ShapeDtypeStruct(pair.shape, BF16), (core, spread(pair, "x"))
    )
    return own, lax.ppermute(own, "core", SWAP)


def compress_sums(core, r, keep, send):
    own, other = sketch_of(core, keep, send)
    n = r.shape[0]
    pieces = lax.axis_size(ROWS)
    rows = 2 * (NG + K) // pieces
    outs = (
        jax.ShapeDtypeStruct((n, K), BF16),
        jax.ShapeDtypeStruct((pieces, rows + 8, NB), BF16),
    )
    scratch = [pltpu.VMEM((NG, NB), F32), pltpu.VMEM((pieces, rows + 8, NB), F32)]
    s, m = call(gram_kernel, "gram", outs, (core, own, other, r), scratch)
    parts = lax.all_to_all(m, ROWS, 0, 0)
    outs = (
        jax.ShapeDtypeStruct((pieces, rows, NB), BF16),
        jax.ShapeDtypeStruct((K, HALF), F32),
    )
    scratch = [pltpu.VMEM((2 * pieces, K), F32), pltpu.VMEM((2 * pieces, HALF), F32)]
    total, corr = call(sum_kernel, "sum", outs, (core, parts), scratch)
    pack = lax.all_to_all(total, ROWS, 0, 0)
    return pack, lax.ppermute(pack, "core", SWAP), corr, s


def per_device(inputs, conv_one, conv_two, probe_one, probe_two):
    n, width = inputs.shape
    pieces = lax.axis_size(ROWS)
    total_rows = n * pieces
    core = lax.axis_index("core").astype(jnp.int32).reshape(1)
    outs = conv_outs(n, width)
    r, keep, send = call(
        first_kernel, "first", outs, (core, inputs, conv_one, probe_one), conv_scratch(n, width)
    )
    sums = compress_sums(core, r, keep, send)
    r, keep, send = call(
        middle_kernel, "middle", outs, (core, *sums, conv_two, probe_two),
        solve_scratch(pieces) + conv_scratch(n, width),
    )
    sums = compress_sums(core, r, keep, send)
    outs = (jax.ShapeDtypeStruct((n, width), BF16), jax.ShapeDtypeStruct((K, K), F32))
    return call(
        functools.partial(last_kernel, 1.0 / math.sqrt(total_rows)), "last", outs, (core, *sums),
        solve_scratch(pieces),
    )


def solution(mesh):
    grid = Mesh(mesh.devices.reshape(8, 4, 4, 2), ("z", "y", "x", "core"))
    rows, chan = ("z", "y"), ("x", "core")
    in_specs = (
        P(rows, chan),
        P(None, None, chan),
        P(None, None, chan),
        P(chan, None),
        P(chan, None),
    )
    out_specs = (P(rows, chan), P())
    return jax.shard_map(
        per_device, mesh=grid, in_specs=in_specs, out_specs=out_specs, check_vma=False
    )
```

```python
import functools
import math

import jax
import jax.numpy as jnp
from jax import lax
from jax.experimental import pallas as pl
from jax.experimental.pallas import tpu as pltpu
from jax.sharding import Mesh, PartitionSpec as P

SIDE = 7
K = 512
NB = 128
HALF = 256
F32 = jnp.float32
BF16 = jnp.bfloat16
VMEM = pl.BlockSpec(memory_space=pltpu.VMEM)
SMEM = pl.BlockSpec(memory_space=pltpu.SMEM)
HBM = pl.BlockSpec(memory_space=pltpu.HBM)
PARAMS = pltpu.CompilerParams(vmem_limit_bytes=48 << 20)
BLOCKS = (((0, 0), (0, 1), (0, 2), (0, 3), (1, 1)), ((1, 2), (1, 3), (2, 2), (2, 3), (3, 3)))
NG = 5 * NB


def dot(a, b, dims=((1,), (0,))):
    return lax.dot_general(a, b, (dims, ((), ())), preferred_element_type=F32)


def bcast_lane(x, k):
    return jnp.broadcast_to(x[:, k : k + 1], (8, NB))


def bcast_row(x, k):
    return jnp.broadcast_to(x[k : k + 1, :], (8, NB))


def combine(coeffs, rows):
    p = [c * b for c, b in zip(coeffs, rows)]
    while len(p) > 1:
        p = [p[i] + p[i + 1] for i in range(0, len(p), 2)]
    return p[0]


def halves(x):
    high = x.astype(BF16)
    return high, (x - high.astype(F32)).astype(BF16)


def factor(rows, side_work):
    n = len(rows)
    sub = lax.broadcasted_iota(jnp.int32, (8, NB), 0)
    lane = lax.broadcasted_iota(jnp.int32, (8, NB), 1)
    at = [sub == i for i in range(8)]
    zero = jnp.zeros((8, NB), F32)
    inv = [(lane == sub + 8 * r).astype(F32) for r in range(n)]
    rows, side_work = list(rows), list(side_work)
    upper, lower_inv = [], []
    for r in range(n):
        top, top_inv = rows[r], inv[r]
        cols = [bcast_lane(top, 8 * r + k) for k in range(8)]
        rb = [bcast_row(top, j) for j in range(8)]
        ib = [bcast_row(top_inv, j) for j in range(8)]
        ldl = [zero] * 8
        d = zero
        for p in range(0, 8, 2):
            a, b, c = bcast_row(cols[p], p), bcast_row(cols[p], p + 1), bcast_row(cols[p + 1], p + 1)
            det = a * c - b * b
            idet, ia = 1.0 / det, 1.0 / a
            ratio, second = b * ia, det * ia
            w0 = cols[p] * c - cols[p + 1] * b
            w1 = cols[p + 1] * a - cols[p] * b
            w0 = jnp.where(at[p], -c, jnp.where(at[p + 1], b, w0))
            w1 = jnp.where(at[p], b, jnp.where(at[p + 1], -a, w1))
            d = jnp.where(at[p], a, jnp.where(at[p + 1], second, d))
            ldl[p] = jnp.where(at[p], a, ldl[p])
            ldl[p + 1] = jnp.where(at[p], b, jnp.where(at[p + 1], second, ldl[p + 1]))
            new = list(cols)
            for j in range(8):
                if j in (p, p + 1):
                    continue
                s0, s1 = bcast_row(cols[j], p), bcast_row(cols[j], p + 1)
                kept = jnp.where(at[p] | at[p + 1], 0.0, cols[j])
                new[j] = kept - (w0 * s0 + w1 * s1) * idet
                if j > p:
                    ldl[j] = jnp.where(at[p], s0, jnp.where(at[p + 1], s1 - ratio * s0, ldl[j]))
            new[p], new[p + 1] = -w0 * idet, -w1 * idet
            cols = new
        x, xi = combine(cols, rb), combine(cols, ib)
        xb = [bcast_row(x, k) for k in range(8)]
        xib = [bcast_row(xi, k) for k in range(8)]
        for g in range(r + 1, n):
            cg = [bcast_lane(rows[g], 8 * r + k) for k in range(8)]
            rows[g], inv[g] = rows[g] - combine(cg, xb), inv[g] - combine(cg, xib)
        q = lax.rsqrt(d)
        upper.append(jnp.where(lane >= 8 * r + sub, q * combine(ldl, xb), 0.0))
        lower_inv.append(q * combine(ldl, xib))
        if r < n - 1:
            k = -(-len(side_work) // (n - 1 - r))
            for work in side_work[:k]:
                work()
            side_work = side_work[k:]
    return jnp.concatenate(upper, axis=0), jnp.concatenate(lower_inv, axis=0)


def solve(a_ref, u_ref, hl_ref, lh_ref, v_ref, x_ref):
    def put(b, lo, hi, value):
        u_ref[b * NB : (b + 1) * NB, lo:hi] = value
        high, low = halves(value)
        for k, part in enumerate((high, low, high)):
            hl_ref[k * NB : (k + 1) * NB, lo:hi] = part
        if lo < K:
            e = min(hi, K)
            for k, part in enumerate((high, high, low)):
                lh_ref[k * NB : (k + 1) * NB, lo:e] = part[:, : e - lo]

    def stack(x):
        high, low = halves(x)
        return jnp.concatenate([high, low, high], axis=0)

    first_inv = K + HALF
    side_work = []
    for b in range(3):
        o, n = b * NB, (b + 1) * NB
        end = first_inv + n
        u, v = factor([a_ref[o + 8 * i : o + 8 * i + 8, o:n] for i in range(16)], side_work)
        u_ref[o:n, o:n] = u
        high, low = halves(v)
        v_ref[...] = jnp.concatenate([high, high, low], axis=1)
        put(b, n, n + NB, dot(v_ref[...], stack(a_ref[o:n, n : n + NB])))
        a_ref[n : n + NB, n : n + NB] -= dot(
            lh_ref[:, n : n + NB], hl_ref[:, n : n + NB], ((0,), (0,))
        )
        put(b, first_inv + o, end, v)

        def rest(b=b, o=o, n=n):
            lo, hi = n + NB, first_inv + o
            put(b, lo, hi, dot(v_ref[...], stack(a_ref[o:n, lo:hi])))

        def trail(r, lo, end=end):
            rows = slice(r * NB, (r + 1) * NB)
            a_ref[rows, lo:end] -= dot(lh_ref[:, rows], hl_ref[:, lo:end], ((0,), (0,)))

        def partial(o=o, n=n, end=end):
            y = u_ref[o:n, K:first_inv].astype(BF16)
            part = dot(
                hl_ref[: 2 * NB, first_inv:end], jnp.concatenate([y, y], axis=0), ((0,), (0,))
            )
            if o:
                x_ref[:o, :] += part[:o]
            x_ref[o:n, :] = part[o:]

        side_work = [rest, functools.partial(trail, b + 1, n + NB)]
        side_work += [functools.partial(trail, r, r * NB) for r in range(b + 2, 4)]
        side_work.append(partial)
    o = 3 * NB
    u, v = factor([a_ref[o + 8 * i : o + 8 * i + 8, o:K] for i in range(16)], side_work)
    u_ref[o:K, o:K] = u
    high, low = halves(v)
    yw = dot(jnp.concatenate([high, high, low], axis=1), stack(a_ref[o:K, K : first_inv + o]))
    y = yw[:, :HALF].astype(BF16)
    high, low = halves(jnp.concatenate([yw[:, HALF:], v], axis=1))
    part = dot(
        jnp.concatenate([high, low], axis=0), jnp.concatenate([y, y], axis=0), ((0,), (0,))
    )
    return jnp.concatenate([x_ref[:o, :] + part[:o], part[o:]], axis=0)


def unpack(pack_ref, t_ref, g_ref, base):
    t_ref[...] = pack_ref[...].astype(F32)
    part = NG // t_ref.shape[0]
    for i in range(t_ref.shape[0]):
        g_ref[pl.ds(base + i * part, part), :] = t_ref[i, :part, :] + t_ref[i, part : 2 * part, :]


def solve_body(core, pack_ref, other_ref, corr_ref, g_ref, t_ref, a_ref, *scratch):
    unpack(other_ref, t_ref, g_ref, (1 - core) * NG)
    unpack(pack_ref, t_ref, g_ref, core * NG)
    pieces = t_ref.shape[0]
    part, step = 2 * NG // pieces, 2 * K // pieces
    blocks = {}
    for c in range(2):
        for n, ij in enumerate(BLOCKS[c]):
            blocks[ij] = (5 * c + n) * NB
    diag = lax.broadcasted_iota(jnp.int32, (NB, NB), 0) == lax.broadcasted_iota(
        jnp.int32, (NB, NB), 1
    )
    root, qrow, qcol = [], [], []
    for b in range(4):
        p = blocks[b, b]
        only = jnp.where(diag, g_ref[p : p + NB, :], 0.0)
        row = jnp.sum(only, axis=0, keepdims=True)
        qrow.append(lax.rsqrt(row))
        qcol.append(lax.rsqrt(jnp.sum(only, axis=1, keepdims=True)))
        root.append(row * qrow[b])
    for (i, j), p in blocks.items():
        a_ref[i * NB : (i + 1) * NB, j * NB : (j + 1) * NB] = (
            g_ref[p : p + NB, :] * qcol[i] * qrow[j]
        )
    for i in range(pieces):
        h, o = divmod(i * step, K)
        rows, lanes = slice(o, o + step), slice(h * NB, (h + 1) * NB)
        a_ref[rows, K + h * NB : K + (h + 1) * NB] = t_ref[i, part:, :] + corr_ref[rows, lanes]
    for b in range(4):
        a_ref[b * NB : (b + 1) * NB, K : K + HALF] *= qcol[b]
    a_ref[:, K + HALF :] = jnp.zeros((K, K), F32)
    x = solve(a_ref, *scratch)
    rows = [(x[b * NB : (b + 1) * NB] * qcol[b]).astype(BF16) for b in range(4)]
    return jnp.concatenate(rows, axis=0), root


def conv_body(core, w_ref, p_ref, r_ref, keep_ref, send_ref, pad_ref, win_ref, bd_ref):
    n = r_ref.shape[0]
    width = r_ref.shape[1]
    group = w_ref.shape[1]
    row = lax.broadcasted_iota(jnp.int32, (n, width), 0)
    q = lax.rem(row, SIDE * SIDE)
    y, x = lax.div(q, SIDE), lax.rem(q, SIDE)
    bi = lax.broadcasted_iota(jnp.int32, (width, width), 0)
    bj = lax.broadcasted_iota(jnp.int32, (width, width), 1)
    same = lax.div(bi, group) == lax.div(bj, group)
    for tap in range(9):
        a, b = tap // 3 - 1, tap % 3 - 1
        d = 8 + a * SIDE + b
        window = pad_ref[d : d + n, :]
        ok = None
        if a:
            ok = (y > 0) if a < 0 else (y < SIDE - 1)
        if b:
            okx = (x > 0) if b < 0 else (x < SIDE - 1)
            ok = okx if ok is None else ok & okx
        if ok is not None:
            window = jnp.where(ok, window, 0.0)
        win_ref[:, tap * width : (tap + 1) * width] = window.astype(BF16)
        tiled = jnp.concatenate([w_ref[tap].astype(F32)] * (width // group), axis=0)
        bd_ref[tap * width : (tap + 1) * width, :] = jnp.where(same, tiled, 0.0).astype(BF16)
    r = dot(win_ref[...], bd_ref[...]).astype(BF16)
    r_ref[...] = r
    mine = pl.multiple_of(core * HALF, HALF)
    theirs = pl.multiple_of((1 - core) * HALF, HALF)
    send_ref[...] = dot(r, p_ref[:, pl.ds(theirs, HALF)]).astype(BF16)
    keep_ref[...] = dot(r, p_ref[:, pl.ds(mine, HALF)])


def pad_field(pad_ref, field):
    n, width = field.shape
    pad_ref[0:8, :] = jnp.zeros((8, width), F32)
    pad_ref[8 + n : 16 + n, :] = jnp.zeros((8, width), F32)
    pad_ref[8 : 8 + n, :] = field


def first_kernel(core_ref, f_hbm, w_hbm, p_hbm, r_ref, keep_ref, send_ref, pad_ref, win_ref, bd_ref,
                 f_ref, w_ref, p_ref, sems):
    copies = [
        pltpu.make_async_copy(src, dst, sems.at[k])
        for k, (src, dst) in enumerate(((w_hbm, w_ref), (f_hbm, f_ref), (p_hbm, p_ref)))
    ]
    for copy in copies:
        copy.start()
    for copy in copies:
        copy.wait()
    pad_field(pad_ref, f_ref[...].astype(F32))
    conv_body(core_ref[0], w_ref, p_ref, r_ref, keep_ref, send_ref, pad_ref, win_ref, bd_ref)


def middle_kernel(core_ref, pack_ref, other_ref, corr_ref, s_ref, w_ref, p_ref, r_ref, keep_ref,
                  send_ref, pad_ref, win_ref, bd_ref, *scratch):
    core = core_ref[0]
    mapped, _ = solve_body(core, pack_ref, other_ref, corr_ref, *scratch)
    restored = dot(s_ref[...], mapped).astype(BF16).astype(F32)
    pad_field(pad_ref, jnp.maximum(restored, 0.0))
    conv_body(core, w_ref, p_ref, r_ref, keep_ref, send_ref, pad_ref, win_ref, bd_ref)


def last_kernel(scale, core_ref, pack_ref, other_ref, corr_ref, s_ref, out_ref, tri_ref, g_ref,
                t_ref, a_ref, u_ref, *scratch):
    mapped, root = solve_body(
        core_ref[0], pack_ref, other_ref, corr_ref, g_ref, t_ref, a_ref, u_ref, *scratch
    )
    out_ref[...] = dot(s_ref[...], mapped).astype(BF16)
    for b in range(4):
        lanes = slice(b * NB, (b + 1) * NB)
        rows = (b + 1) * NB
        tri_ref[:rows, lanes] = u_ref[:rows, lanes] * (root[b] * scale)
        if rows < K:
            tri_ref[rows:, lanes] = jnp.zeros((K - rows, NB), F32)


def gram_kernel(core_ref, own_ref, other_ref, r_ref, s_ref, m_ref, g_ref, t_ref):
    core = core_ref[0]
    n = own_ref.shape[0]
    pieces = t_ref.shape[0]
    s_ref[:, pl.ds(pl.multiple_of(core * HALF, HALF), HALF)] = own_ref[...]
    s_ref[:, pl.ds(pl.multiple_of((1 - core) * HALF, HALF), HALF)] = other_ref[...]
    s, r = s_ref[...], r_ref[...]
    ones = jnp.ones((8, n), BF16)
    mean = (dot(ones, s) * (1.0 / n)).astype(BF16).astype(F32)
    total = dot(ones, r)
    high = total.astype(BF16).astype(F32)
    low = (total - high).astype(BF16).astype(F32)
    first = lax.broadcasted_iota(jnp.int32, (8, K), 0) < 1
    left = jnp.where(lax.broadcasted_iota(jnp.int32, (8, K), 0) < 2, mean, 0.0).astype(BF16)
    right = jnp.where(first[:, :HALF], high, low).astype(BF16)
    cross = dot(s, r, ((0,), (0,))) - dot(left, right, ((0,), (0,)))
    extra = jnp.concatenate(
        [mean[:1, h * NB : (h + 1) * NB] for h in range(4)]
        + [high[:1, h * NB : (h + 1) * NB] for h in range(2)]
        + [low[:1, h * NB : (h + 1) * NB] for h in range(2)],
        axis=0,
    )
    for c in range(2):

        @pl.when(core == c)
        def _():
            for k, (i, j) in enumerate(BLOCKS[c]):
                block = dot(
                    s_ref[:, i * NB : (i + 1) * NB], s_ref[:, j * NB : (j + 1) * NB], ((0,), (0,))
                )
                g_ref[k * NB : (k + 1) * NB, :] = block

    part = NG // pieces
    step = 2 * K // pieces
    for i in range(pieces):
        g = g_ref[i * part : (i + 1) * part, :]
        hi = g.astype(BF16).astype(F32)
        t_ref[i, :part, :] = hi
        t_ref[i, part : 2 * part, :] = g - hi
        h, o = divmod(i * step, K)
        t_ref[i, 2 * part : 2 * part + step, :] = cross[o : o + step, h * NB : (h + 1) * NB]
        t_ref[i, 2 * part + step :, :] = extra
    m_ref[...] = t_ref[...].astype(BF16)


def sum_kernel(core_ref, parts_ref, out_ref, corr_ref, left_ref, right_ref):
    pieces, rows = parts_ref.shape[:2]
    part = NG // pieces
    keep = rows - 8
    acc = parts_ref[0, :keep, :].astype(F32)
    for i in range(1, pieces):
        acc = acc + parts_ref[i, :keep, :].astype(F32)
    g = acc[:part] + acc[part : 2 * part]
    hi = g.astype(BF16).astype(F32)
    total = jnp.concatenate([hi, g - hi, acc[2 * part :]], axis=0).astype(BF16)
    for i in range(pieces):
        out_ref[i] = total
    for i in range(pieces):
        e = parts_ref[i, keep:, :].astype(F32)
        for h in range(4):
            for k in range(2):
                left_ref[pieces * k + i : pieces * k + i + 1, h * NB : (h + 1) * NB] = e[h : h + 1]
        for h in range(2):
            for k in range(2):
                right_ref[pieces * k + i : pieces * k + i + 1, h * NB : (h + 1) * NB] = e[
                    4 + 2 * k + h : 5 + 2 * k + h
                ]
    corr_ref[...] = dot(left_ref[...].astype(BF16), right_ref[...].astype(BF16), ((0,), (0,)))


def fold_kernel(core_ref, parts_ref, out_ref):
    acc = parts_ref[0].astype(F32)
    for i in range(1, parts_ref.shape[0]):
        acc = acc + parts_ref[i].astype(F32)
    out_ref[...] = acc.astype(BF16)


def solve_scratch(pieces):
    total = 2 * K + HALF
    return [
        pltpu.VMEM((2 * NG, NB), F32),
        pltpu.VMEM((pieces, 2 * (NG + K) // pieces, NB), F32),
        pltpu.VMEM((K, total), F32),
        pltpu.VMEM((K, total), F32),
        pltpu.VMEM((3 * NB, total), BF16),
        pltpu.VMEM((3 * NB, K), BF16),
        pltpu.VMEM((NB, 3 * NB), BF16),
        pltpu.VMEM((K, HALF), F32),
    ]


def conv_scratch(n, width):
    return [
        pltpu.VMEM((n + 16, width), F32),
        pltpu.VMEM((n, 9 * width), BF16),
        pltpu.VMEM((9 * width, width), BF16),
    ]


def conv_outs(n, width):
    return (
        jax.ShapeDtypeStruct((n, width), BF16),
        jax.ShapeDtypeStruct((n, HALF), F32),
        jax.ShapeDtypeStruct((n, HALF), BF16),
    )


def call(kernel, name, outs, args, scratch=(), space=VMEM):
    return pl.pallas_call(
        kernel,
        out_shape=outs,
        in_specs=[SMEM] + [space] * (len(args) - 1),
        out_specs=jax.tree.map(lambda _: VMEM, outs),
        scratch_shapes=list(scratch),
        compiler_params=PARAMS,
        name=name,
    )(*args)


SWAP = ((0, 1), (1, 0))
ROWS = ("z", "y")


def spread(x, axes):
    n = lax.axis_size(axes)
    return lax.all_to_all(jnp.broadcast_to(x[None], (n,) + x.shape), axes, 0, 0)


def sketch_of(core, keep, send):
    pair = (keep + lax.ppermute(send, "core", SWAP).astype(F32)).astype(BF16)
    own = call(
        fold_kernel, "fold", jax.ShapeDtypeStruct(pair.shape, BF16), (core, spread(pair, "x"))
    )
    return own, lax.ppermute(own, "core", SWAP)


def compress_sums(core, r, keep, send):
    own, other = sketch_of(core, keep, send)
    n = r.shape[0]
    pieces = lax.axis_size(ROWS)
    rows = 2 * (NG + K) // pieces
    outs = (
        jax.ShapeDtypeStruct((n, K), BF16),
        jax.ShapeDtypeStruct((pieces, rows + 8, NB), BF16),
    )
    scratch = [pltpu.VMEM((NG, NB), F32), pltpu.VMEM((pieces, rows + 8, NB), F32)]
    s, m = call(gram_kernel, "gram", outs, (core, own, other, r), scratch)
    parts = lax.all_to_all(m, ROWS, 0, 0)
    outs = (
        jax.ShapeDtypeStruct((pieces, rows, NB), BF16),
        jax.ShapeDtypeStruct((K, HALF), F32),
    )
    scratch = [pltpu.VMEM((2 * pieces, K), F32), pltpu.VMEM((2 * pieces, HALF), F32)]
    total, corr = call(sum_kernel, "sum", outs, (core, parts), scratch)
    pack = lax.all_to_all(total, ROWS, 0, 0)
    return pack, lax.ppermute(pack, "core", SWAP), corr, s


def per_device(inputs, conv_one, conv_two, probe_one, probe_two):
    n, width = inputs.shape
    pieces = lax.axis_size(ROWS)
    total_rows = n * pieces
    core = lax.axis_index("core").astype(jnp.int32).reshape(1)
    outs = conv_outs(n, width)
    args = (inputs, conv_one, probe_one)
    scratch = conv_scratch(n, width) + [pltpu.VMEM(x.shape, x.dtype) for x in args]
    scratch.append(pltpu.SemaphoreType.DMA((len(args),)))
    pinned = [pltpu.with_memory_space_constraint(x, pltpu.HBM) for x in args]
    r, keep, send = call(first_kernel, "first", outs, (core, *pinned), scratch, HBM)
    sums = compress_sums(core, r, keep, send)
    r, keep, send = call(
        middle_kernel, "middle", outs, (core, *sums, conv_two, probe_two),
        conv_scratch(n, width) + solve_scratch(pieces),
    )
    sums = compress_sums(core, r, keep, send)
    outs = (jax.ShapeDtypeStruct((n, width), BF16), jax.ShapeDtypeStruct((K, K), F32))
    return call(
        functools.partial(last_kernel, 1.0 / math.sqrt(total_rows)), "last", outs, (core, *sums),
        solve_scratch(pieces),
    )


def solution(mesh):
    grid = Mesh(mesh.devices.reshape(8, 4, 4, 2), ("z", "y", "x", "core"))
    rows, chan = ("z", "y"), ("x", "core")
    in_specs = (
        P(rows, chan),
        P(None, None, chan),
        P(None, None, chan),
        P(chan, None),
        P(chan, None),
    )
    out_specs = (P(rows, chan), P())
    return jax.shard_map(
        per_device, mesh=grid, in_specs=in_specs, out_specs=out_specs, check_vma=False
    )
```

```python
import functools
import math

import jax
import jax.numpy as jnp
from jax import lax
from jax.experimental import pallas as pl
from jax.experimental.pallas import tpu as pltpu
from jax.sharding import Mesh, PartitionSpec as P

SIDE = 7
K = 512
NB = 128
HALF = 256
F32 = jnp.float32
BF16 = jnp.bfloat16
VMEM = pl.BlockSpec(memory_space=pltpu.VMEM)
SMEM = pl.BlockSpec(memory_space=pltpu.SMEM)
HBM = pl.BlockSpec(memory_space=pltpu.HBM)
PARAMS = pltpu.CompilerParams(vmem_limit_bytes=48 << 20)
BLOCKS = (((0, 0), (0, 1), (0, 2), (0, 3), (1, 1)), ((1, 2), (1, 3), (2, 2), (2, 3), (3, 3)))
NG = 5 * NB
SEND = 64


def dot(a, b, dims=((1,), (0,))):
    return lax.dot_general(a, b, (dims, ((), ())), preferred_element_type=F32)


def bcast_lane(x, k):
    return jnp.broadcast_to(x[:, k : k + 1], (8, NB))


def bcast_row(x, k):
    return jnp.broadcast_to(x[k : k + 1, :], (8, NB))


def combine(coeffs, rows):
    p = [c * b for c, b in zip(coeffs, rows)]
    while len(p) > 1:
        p = [p[i] + p[i + 1] for i in range(0, len(p), 2)]
    return p[0]


def halves(x):
    high = x.astype(BF16)
    return high, (x - high.astype(F32)).astype(BF16)


def factor(rows, side_work):
    n = len(rows)
    sub = lax.broadcasted_iota(jnp.int32, (8, NB), 0)
    lane = lax.broadcasted_iota(jnp.int32, (8, NB), 1)
    at = [sub == i for i in range(8)]
    zero = jnp.zeros((8, NB), F32)
    inv = [(lane == sub + 8 * r).astype(F32) for r in range(n)]
    rows, side_work = list(rows), list(side_work)
    upper, lower_inv = [], []
    for r in range(n):
        top, top_inv = rows[r], inv[r]
        cols = [bcast_lane(top, 8 * r + k) for k in range(8)]
        rb = [bcast_row(top, j) for j in range(8)]
        ib = [bcast_row(top_inv, j) for j in range(8)]
        ldl = [zero] * 8
        d = zero
        for p in range(0, 8, 2):
            a, b, c = bcast_row(cols[p], p), bcast_row(cols[p], p + 1), bcast_row(cols[p + 1], p + 1)
            det = a * c - b * b
            idet, ia = 1.0 / det, 1.0 / a
            ratio, second = b * ia, det * ia
            w0 = cols[p] * c - cols[p + 1] * b
            w1 = cols[p + 1] * a - cols[p] * b
            w0 = jnp.where(at[p], -c, jnp.where(at[p + 1], b, w0))
            w1 = jnp.where(at[p], b, jnp.where(at[p + 1], -a, w1))
            d = jnp.where(at[p], a, jnp.where(at[p + 1], second, d))
            ldl[p] = jnp.where(at[p], a, ldl[p])
            ldl[p + 1] = jnp.where(at[p], b, jnp.where(at[p + 1], second, ldl[p + 1]))
            new = list(cols)
            for j in range(8):
                if j in (p, p + 1):
                    continue
                s0, s1 = bcast_row(cols[j], p), bcast_row(cols[j], p + 1)
                kept = jnp.where(at[p] | at[p + 1], 0.0, cols[j])
                new[j] = kept - (w0 * s0 + w1 * s1) * idet
                if j > p:
                    ldl[j] = jnp.where(at[p], s0, jnp.where(at[p + 1], s1 - ratio * s0, ldl[j]))
            new[p], new[p + 1] = -w0 * idet, -w1 * idet
            cols = new
        x, xi = combine(cols, rb), combine(cols, ib)
        xb = [bcast_row(x, k) for k in range(8)]
        xib = [bcast_row(xi, k) for k in range(8)]
        for g in range(r + 1, n):
            cg = [bcast_lane(rows[g], 8 * r + k) for k in range(8)]
            rows[g], inv[g] = rows[g] - combine(cg, xb), inv[g] - combine(cg, xib)
        q = lax.rsqrt(d)
        upper.append(jnp.where(lane >= 8 * r + sub, q * combine(ldl, xb), 0.0))
        lower_inv.append(q * combine(ldl, xib))
        if r < n - 1:
            k = -(-len(side_work) // (n - 1 - r))
            for work in side_work[:k]:
                work()
            side_work = side_work[k:]
    return jnp.concatenate(upper, axis=0), jnp.concatenate(lower_inv, axis=0)


def solve(early, late, a_ref, u_ref, hl_ref, lh_ref, v_ref, x_ref):
    def put(b, lo, hi, value):
        u_ref[b * NB : (b + 1) * NB, lo:hi] = value
        high, low = halves(value)
        for k, part in enumerate((high, low, high)):
            hl_ref[k * NB : (k + 1) * NB, lo:hi] = part
        if lo < K:
            e = min(hi, K)
            for k, part in enumerate((high, high, low)):
                lh_ref[k * NB : (k + 1) * NB, lo:e] = part[:, : e - lo]

    def stack(x):
        high, low = halves(x)
        return jnp.concatenate([high, low, high], axis=0)

    first_inv = K + HALF
    side_work = early
    for b in range(3):
        o, n = b * NB, (b + 1) * NB
        end = first_inv + n
        u, v = factor([a_ref[o + 8 * i : o + 8 * i + 8, o:n] for i in range(16)], side_work)
        u_ref[o:n, o:n] = u
        high, low = halves(v)
        v_ref[...] = jnp.concatenate([high, high, low], axis=1)
        put(b, n, n + NB, dot(v_ref[...], stack(a_ref[o:n, n : n + NB])))
        a_ref[n : n + NB, n : n + NB] -= dot(
            lh_ref[:, n : n + NB], hl_ref[:, n : n + NB], ((0,), (0,))
        )
        put(b, first_inv + o, end, v)

        def rest(b=b, o=o, n=n):
            lo, hi = n + NB, first_inv + o
            put(b, lo, hi, dot(v_ref[...], stack(a_ref[o:n, lo:hi])))

        def trail(r, lo, end=end):
            rows = slice(r * NB, (r + 1) * NB)
            a_ref[rows, lo:end] -= dot(lh_ref[:, rows], hl_ref[:, lo:end], ((0,), (0,)))

        def partial(o=o, n=n, end=end):
            y = u_ref[o:n, K:first_inv].astype(BF16)
            part = dot(
                hl_ref[: 2 * NB, first_inv:end], jnp.concatenate([y, y], axis=0), ((0,), (0,))
            )
            if o:
                x_ref[:o, :] += part[:o]
            x_ref[o:n, :] = part[o:]

        side_work = [rest, functools.partial(trail, b + 1, n + NB)]
        side_work += [functools.partial(trail, r, r * NB) for r in range(b + 2, 4)]
        side_work.append(partial)
    o = 3 * NB
    side_work += late
    u, v = factor([a_ref[o + 8 * i : o + 8 * i + 8, o:K] for i in range(16)], side_work)
    u_ref[o:K, o:K] = u
    high, low = halves(v)
    yw = dot(jnp.concatenate([high, high, low], axis=1), stack(a_ref[o:K, K : first_inv + o]))
    y = yw[:, :HALF].astype(BF16)
    high, low = halves(jnp.concatenate([yw[:, HALF:], v], axis=1))
    part = dot(
        jnp.concatenate([high, low], axis=0), jnp.concatenate([y, y], axis=0), ((0,), (0,))
    )
    return jnp.concatenate([x_ref[:o, :] + part[:o], part[o:]], axis=0)


def solve_body(core, pack_ref, other_ref, corr_ref, left_ref, count, late, g_ref, t_ref, a_ref,
               *scratch):
    pieces = pack_ref.shape[0]
    part, step = NG // pieces, 2 * K // pieces
    where = {ij: (c, n * NB) for c in range(2) for n, ij in enumerate(BLOCKS[c])}
    diag = lax.broadcasted_iota(jnp.int32, (NB, NB), 0) == lax.broadcasted_iota(
        jnp.int32, (NB, NB), 1
    )
    ready = set()
    root, qrow, qcol = [None] * 4, [None] * 4, [None] * 4

    def unpack(c, p):
        for i in range(p // part, (p + NB - 1) // part + 1):
            if (c, i) not in ready:
                ready.add((c, i))
                mine, theirs = pack_ref[i].astype(F32), other_ref[i].astype(F32)
                t_ref[i] = jnp.where(core == c, mine, theirs)
                q = c * NG + i * part
                g_ref[q : q + part, :] = t_ref[i, :part, :] + t_ref[i, part : 2 * part, :]

    def block(i, j):
        c, p = where[i, j]
        unpack(c, p)
        mean = dot(
            left_ref[:pieces, i * NB : (i + 1) * NB],
            left_ref[:pieces, j * NB : (j + 1) * NB],
            ((0,), (0,)),
        )
        return g_ref[c * NG + p : c * NG + p + NB, :] + count * mean

    def diagonal(b):
        g = block(b, b)
        only = jnp.where(diag, g, 0.0)
        row = jnp.sum(only, axis=0, keepdims=True)
        qrow[b] = lax.rsqrt(row)
        qcol[b] = lax.rsqrt(jnp.sum(only, axis=1, keepdims=True))
        root[b] = row * qrow[b]
        rows = slice(b * NB, (b + 1) * NB)
        a_ref[rows, rows] = g * qcol[b] * qrow[b]

    def off_diagonal(i, j):
        a_ref[i * NB : (i + 1) * NB, j * NB : (j + 1) * NB] = block(i, j) * qcol[i] * qrow[j]

    def right_side(b):
        rows = slice(b * NB, (b + 1) * NB)
        for h in range(2):
            for o in range(b * NB, (b + 1) * NB, step):
                i = (h * K + o) // step
                lanes = slice(K + h * NB, K + (h + 1) * NB)
                c = pack_ref[i].astype(F32)[2 * part :]
                a_ref[o : o + step, lanes] = c + corr_ref[o : o + step, h * NB : (h + 1) * NB]
        a_ref[rows, K : K + HALF] *= qcol[b]
        a_ref[rows, K + HALF :] = jnp.zeros((NB, K), F32)

    diagonal(0)
    early = [functools.partial(diagonal, b) for b in range(1, 4)]
    early += [functools.partial(off_diagonal, i, j) for i in range(4) for j in range(i + 1, 4)]
    early += [functools.partial(right_side, b) for b in range(4)]
    x = solve(early, late, a_ref, *scratch)
    rows = [(x[b * NB : (b + 1) * NB] * qcol[b]).astype(BF16) for b in range(4)]
    return jnp.concatenate(rows, axis=0), root


def block_weights(w_ref, bd_ref):
    group, width = w_ref.shape[1:]

    def write(tap):
        bi = lax.broadcasted_iota(jnp.int32, (width, width), 0)
        bj = lax.broadcasted_iota(jnp.int32, (width, width), 1)
        tiled = jnp.concatenate([w_ref[tap].astype(F32)] * (width // group), axis=0)
        same = lax.div(bi, group) == lax.div(bj, group)
        bd_ref[tap * width : (tap + 1) * width, :] = jnp.where(same, tiled, 0.0).astype(BF16)

    return [functools.partial(write, tap) for tap in range(9)]


def conv_body(core, p_ref, r_ref, keep_ref, send_ref, pad_ref, win_ref, bd_ref):
    n = r_ref.shape[0]
    width = r_ref.shape[1]
    row = lax.broadcasted_iota(jnp.int32, (n, width), 0)
    q = lax.rem(row, SIDE * SIDE)
    y, x = lax.div(q, SIDE), lax.rem(q, SIDE)
    for tap in range(9):
        a, b = tap // 3 - 1, tap % 3 - 1
        d = 8 + a * SIDE + b
        window = pad_ref[d : d + n, :]
        ok = None
        if a:
            ok = (y > 0) if a < 0 else (y < SIDE - 1)
        if b:
            okx = (x > 0) if b < 0 else (x < SIDE - 1)
            ok = okx if ok is None else ok & okx
        if ok is not None:
            window = jnp.where(ok, window, 0.0)
        win_ref[:, tap * width : (tap + 1) * width] = window.astype(BF16)
    r = dot(win_ref[...], bd_ref[...]).astype(BF16)
    r_ref[...] = r
    mine = pl.multiple_of(core * HALF, HALF)
    theirs = pl.multiple_of((1 - core) * HALF, HALF)
    send_ref[...] = dot(r, p_ref[:, pl.ds(theirs, HALF)]).astype(BF16)
    keep_ref[...] = dot(r, p_ref[:, pl.ds(mine, HALF)])


def pad_field(pad_ref, field):
    n, width = field.shape
    pad_ref[0:8, :] = jnp.zeros((8, width), F32)
    pad_ref[8 + n : 16 + n, :] = jnp.zeros((8, width), F32)
    pad_ref[8 : 8 + n, :] = field


def first_kernel(core_ref, f_hbm, w_hbm, p_hbm, r_ref, keep_ref, send_ref, pad_ref, win_ref, bd_ref,
                 f_ref, w_ref, p_ref, sems):
    copies = [
        pltpu.make_async_copy(src, dst, sems.at[k])
        for k, (src, dst) in enumerate(((w_hbm, w_ref), (f_hbm, f_ref), (p_hbm, p_ref)))
    ]
    for copy in copies:
        copy.start()
    copies[0].wait()
    for write in block_weights(w_ref, bd_ref):
        write()
    copies[1].wait()
    pad_field(pad_ref, f_ref[...].astype(F32))
    copies[2].wait()
    conv_body(core_ref[0], p_ref, r_ref, keep_ref, send_ref, pad_ref, win_ref, bd_ref)


def middle_kernel(count, core_ref, pack_ref, other_ref, corr_ref, left_ref, s_ref, w_ref, p_ref,
                  r_ref, keep_ref, send_ref, pad_ref, win_ref, bd_ref, *scratch):
    core = core_ref[0]
    late = block_weights(w_ref, bd_ref)
    mapped, _ = solve_body(
        core, pack_ref, other_ref, corr_ref, left_ref, count, late, *scratch
    )
    restored = dot(s_ref[...], mapped).astype(BF16).astype(F32)
    pad_field(pad_ref, jnp.maximum(restored, 0.0))
    conv_body(core, p_ref, r_ref, keep_ref, send_ref, pad_ref, win_ref, bd_ref)


def last_kernel(count, scale, core_ref, pack_ref, other_ref, corr_ref, left_ref, s_ref, out_ref,
                tri_ref, g_ref, t_ref, a_ref, u_ref, *scratch):
    mapped, root = solve_body(
        core_ref[0], pack_ref, other_ref, corr_ref, left_ref, count, [], g_ref, t_ref, a_ref,
        u_ref, *scratch,
    )
    out_ref[...] = dot(s_ref[...], mapped).astype(BF16)
    for b in range(4):
        lanes = slice(b * NB, (b + 1) * NB)
        rows = (b + 1) * NB
        tri_ref[:rows, lanes] = u_ref[:rows, lanes] * (root[b] * scale)
        if rows < K:
            tri_ref[rows:, lanes] = jnp.zeros((K - rows, NB), F32)


def gram_kernel(core_ref, own_ref, other_ref, r_ref, s_ref, m_ref, g_ref, t_ref):
    core = core_ref[0]
    n = own_ref.shape[0]
    pieces = t_ref.shape[0]
    s_ref[:, pl.ds(pl.multiple_of(core * HALF, HALF), HALF)] = own_ref[...]
    s_ref[:, pl.ds(pl.multiple_of((1 - core) * HALF, HALF), HALF)] = other_ref[...]
    s, r = s_ref[...], r_ref[...]
    ones = jnp.ones((8, n), BF16)
    mean = (dot(ones, s) * (1.0 / n)).astype(BF16).astype(F32)
    total = dot(ones, r)
    high = total.astype(BF16).astype(F32)
    low = (total - high).astype(BF16).astype(F32)
    first = lax.broadcasted_iota(jnp.int32, (8, K), 0) < 1
    left = jnp.where(lax.broadcasted_iota(jnp.int32, (8, K), 0) < 2, mean, 0.0).astype(BF16)
    only = jnp.where(first, mean, 0.0).astype(BF16)
    right = jnp.where(first[:, :HALF], high, low).astype(BF16)
    cross = dot(s, r, ((0,), (0,))) - dot(left, right, ((0,), (0,)))
    extra = jnp.concatenate(
        [mean[:1, h * NB : (h + 1) * NB] for h in range(4)]
        + [high[:1, h * NB : (h + 1) * NB] for h in range(2)]
        + [low[:1, h * NB : (h + 1) * NB] for h in range(2)],
        axis=0,
    )
    for c in range(2):

        @pl.when(core == c)
        def _():
            for k, (i, j) in enumerate(BLOCKS[c]):
                a, b = slice(i * NB, (i + 1) * NB), slice(j * NB, (j + 1) * NB)
                block = dot(s_ref[:, a], s_ref[:, b], ((0,), (0,)))
                g_ref[k * NB : (k + 1) * NB, :] = block - n * dot(
                    only[:, a], only[:, b], ((0,), (0,))
                )

    part = NG // pieces
    step = 2 * K // pieces
    for i in range(pieces):
        t_ref[i, :part, :] = g_ref[i * part : (i + 1) * part, :]
        h, o = divmod(i * step, K)
        t_ref[i, part : part + step, :] = cross[o : o + step, h * NB : (h + 1) * NB]
        t_ref[i, part + step : part + step + 8, :] = extra
        t_ref[i, part + step + 8 :, :] = jnp.zeros((SEND - part - step - 8, NB), F32)
    m_ref[...] = t_ref[...].astype(BF16)


def sum_kernel(core_ref, parts_ref, out_ref, corr_ref, left_ref, l_ref, right_ref):
    pieces = parts_ref.shape[0]
    part, step = NG // pieces, 2 * K // pieces
    acc = None
    for i in range(pieces):
        piece = parts_ref[i].astype(F32)
        acc = piece if acc is None else acc + piece
        e = piece[part + step : part + step + 8]
        for k in range(2):
            q = pieces * k + i
            for h in range(4):
                l_ref[q : q + 1, h * NB : (h + 1) * NB] = e[h : h + 1]
            for h in range(2):
                right_ref[q : q + 1, h * NB : (h + 1) * NB] = e[4 + 2 * k + h : 5 + 2 * k + h]
    g = acc[:part]
    hi = g.astype(BF16).astype(F32)
    total = jnp.concatenate([hi, g - hi, acc[part : part + step]], axis=0).astype(BF16)
    for i in range(pieces):
        out_ref[i] = total
    left = l_ref[...].astype(BF16)
    left_ref[...] = left
    corr_ref[...] = dot(left, right_ref[...].astype(BF16), ((0,), (0,)))


def fold_kernel(core_ref, parts_ref, out_ref):
    acc = parts_ref[0].astype(F32)
    for i in range(1, parts_ref.shape[0]):
        acc = acc + parts_ref[i].astype(F32)
    out_ref[...] = acc.astype(BF16)


def solve_scratch(pieces):
    total = 2 * K + HALF
    return [
        pltpu.VMEM((2 * NG, NB), F32),
        pltpu.VMEM((pieces, 2 * (NG + K) // pieces, NB), F32),
        pltpu.VMEM((K, total), F32),
        pltpu.VMEM((K, total), F32),
        pltpu.VMEM((3 * NB, total), BF16),
        pltpu.VMEM((3 * NB, K), BF16),
        pltpu.VMEM((NB, 3 * NB), BF16),
        pltpu.VMEM((K, HALF), F32),
    ]


def conv_scratch(n, width):
    return [
        pltpu.VMEM((n + 16, width), F32),
        pltpu.VMEM((n, 9 * width), BF16),
        pltpu.VMEM((9 * width, width), BF16),
    ]


def conv_outs(n, width):
    return (
        jax.ShapeDtypeStruct((n, width), BF16),
        jax.ShapeDtypeStruct((n, HALF), F32),
        jax.ShapeDtypeStruct((n, HALF), BF16),
    )


def call(kernel, name, outs, args, scratch=(), space=VMEM):
    return pl.pallas_call(
        kernel,
        out_shape=outs,
        in_specs=[SMEM] + [space] * (len(args) - 1),
        out_specs=jax.tree.map(lambda _: VMEM, outs),
        scratch_shapes=list(scratch),
        compiler_params=PARAMS,
        name=name,
    )(*args)


SWAP = ((0, 1), (1, 0))
ROWS = ("z", "y")


def spread(x, axes):
    n = lax.axis_size(axes)
    return lax.all_to_all(jnp.broadcast_to(x[None], (n,) + x.shape), axes, 0, 0)


def sketch_of(core, keep, send):
    pair = (keep + lax.ppermute(send, "core", SWAP).astype(F32)).astype(BF16)
    own = call(
        fold_kernel, "fold", jax.ShapeDtypeStruct(pair.shape, BF16), (core, spread(pair, "x"))
    )
    return own, lax.ppermute(own, "core", SWAP)


def compress_sums(core, r, keep, send):
    own, other = sketch_of(core, keep, send)
    n = r.shape[0]
    pieces = lax.axis_size(ROWS)
    rows = 2 * (NG + K) // pieces
    outs = (
        jax.ShapeDtypeStruct((n, K), BF16),
        jax.ShapeDtypeStruct((pieces, SEND, NB), BF16),
    )
    scratch = [pltpu.VMEM((NG, NB), F32), pltpu.VMEM((pieces, SEND, NB), F32)]
    s, m = call(gram_kernel, "gram", outs, (core, own, other, r), scratch)
    parts = lax.all_to_all(m, ROWS, 0, 0)
    outs = (
        jax.ShapeDtypeStruct((pieces, rows, NB), BF16),
        jax.ShapeDtypeStruct((K, HALF), F32),
        jax.ShapeDtypeStruct((2 * pieces, K), BF16),
    )
    scratch = [pltpu.VMEM((2 * pieces, K), F32), pltpu.VMEM((2 * pieces, HALF), F32)]
    total, corr, left = call(sum_kernel, "sum", outs, (core, parts), scratch)
    pack = lax.all_to_all(total, ROWS, 0, 0)
    return pack, lax.ppermute(pack, "core", SWAP), corr, left, s


def per_device(inputs, conv_one, conv_two, probe_one, probe_two):
    n, width = inputs.shape
    pieces = lax.axis_size(ROWS)
    total_rows = n * pieces
    core = lax.axis_index("core").astype(jnp.int32).reshape(1)
    outs = conv_outs(n, width)
    args = (inputs, conv_one, probe_one)
    scratch = conv_scratch(n, width) + [pltpu.VMEM(x.shape, x.dtype) for x in args]
    scratch.append(pltpu.SemaphoreType.DMA((len(args),)))
    pinned = [pltpu.with_memory_space_constraint(x, pltpu.HBM) for x in args]
    r, keep, send = call(first_kernel, "first", outs, (core, *pinned), scratch, HBM)
    sums = compress_sums(core, r, keep, send)
    r, keep, send = call(
        functools.partial(middle_kernel, n), "middle", outs, (core, *sums, conv_two, probe_two),
        conv_scratch(n, width) + solve_scratch(pieces),
    )
    sums = compress_sums(core, r, keep, send)
    outs = (jax.ShapeDtypeStruct((n, width), BF16), jax.ShapeDtypeStruct((K, K), F32))
    return call(
        functools.partial(last_kernel, n, 1.0 / math.sqrt(total_rows)), "last", outs, (core, *sums),
        solve_scratch(pieces),
    )


def solution(mesh):
    grid = Mesh(mesh.devices.reshape(8, 4, 4, 2), ("z", "y", "x", "core"))
    rows, chan = ("z", "y"), ("x", "core")
    in_specs = (
        P(rows, chan),
        P(None, None, chan),
        P(None, None, chan),
        P(chan, None),
        P(chan, None),
    )
    out_specs = (P(rows, chan), P())
    return jax.shard_map(
        per_device, mesh=grid, in_specs=in_specs, out_specs=out_specs, check_vma=False
    )
```

```python
import functools
import math

import jax
import jax.numpy as jnp
from jax import lax
from jax.experimental import pallas as pl
from jax.experimental.pallas import tpu as pltpu
from jax.sharding import Mesh, PartitionSpec as P

SIDE = 7
K = 512
NB = 128
HALF = 256
F32 = jnp.float32
BF16 = jnp.bfloat16
VMEM = pl.BlockSpec(memory_space=pltpu.VMEM)
SMEM = pl.BlockSpec(memory_space=pltpu.SMEM)
HBM = pl.BlockSpec(memory_space=pltpu.HBM)
PARAMS = pltpu.CompilerParams(vmem_limit_bytes=48 << 20)
BLOCKS = (((0, 0), (0, 1), (0, 2), (0, 3), (1, 1)), ((1, 2), (1, 3), (2, 2), (2, 3), (3, 3)))
NG = 5 * NB
SEND = 64
RETURN = 56


def dot(a, b, dims=((1,), (0,))):
    return lax.dot_general(a, b, (dims, ((), ())), preferred_element_type=F32)


def bcast_lane(x, k):
    return jnp.broadcast_to(x[:, k : k + 1], (8, NB))


def bcast_row(x, k):
    return jnp.broadcast_to(x[k : k + 1, :], (8, NB))


def combine(coeffs, rows):
    p = [c * b for c, b in zip(coeffs, rows)]
    while len(p) > 1:
        p = [p[i] + p[i + 1] for i in range(0, len(p), 2)]
    return p[0]


def halves(x):
    high = x.astype(BF16)
    return high, (x - high.astype(F32)).astype(BF16)


def factor(rows, side_work):
    n = len(rows)
    sub = lax.broadcasted_iota(jnp.int32, (8, NB), 0)
    lane = lax.broadcasted_iota(jnp.int32, (8, NB), 1)
    at = [sub == i for i in range(8)]
    zero = jnp.zeros((8, NB), F32)
    unit = [(sub == i).astype(F32) for i in range(8)]
    inv = [(lane == sub + 8 * r).astype(F32) for r in range(n)]
    rows, side_work = list(rows), list(side_work)
    upper, lower_inv = [], []
    for r in range(n):
        top, top_inv = rows[r], inv[r]
        cols = [bcast_lane(top, 8 * r + k) for k in range(8)]
        rb = [bcast_row(top, j) for j in range(8)]
        ib = [bcast_row(top_inv, j) for j in range(8)]
        pivots = []
        for p in range(0, 8, 2):
            a, b, c = bcast_row(cols[p], p), bcast_row(cols[p], p + 1), bcast_row(cols[p + 1], p + 1)
            det = a * c - b * b
            idet = 1.0 / det
            w0 = cols[p] * c - cols[p + 1] * b
            w1 = cols[p + 1] * a - cols[p] * b
            w0 = jnp.where(at[p], det - c, jnp.where(at[p + 1], b, w0))
            w1 = jnp.where(at[p], b, jnp.where(at[p + 1], det - a, w1))
            z0, z1 = w0 * idet, w1 * idet
            new, above = list(cols), {}
            for j in range(8):
                if j in (p, p + 1):
                    continue
                s0, s1 = bcast_row(cols[j], p), bcast_row(cols[j], p + 1)
                if j in (p + 2, p + 3):
                    new[j] = cols[j] - (w0 * s0 + w1 * s1) * idet
                else:
                    new[j] = cols[j] - (z0 * s0 + z1 * s1)
                if j > p:
                    above[j] = (s0, s1)
            new[p], new[p + 1] = unit[p] - z0, unit[p + 1] - z1
            pivots.append((p, a, b, det, above))
            cols = new
        x, xi = combine(cols, rb), combine(cols, ib)
        xb = [bcast_row(x, k) for k in range(8)]
        xib = [bcast_row(xi, k) for k in range(8)]
        for g in range(r + 1, n):
            cg = [bcast_lane(rows[g], 8 * r + k) for k in range(8)]
            rows[g], inv[g] = rows[g] - combine(cg, xb), inv[g] - combine(cg, xib)
        ldl, d = [zero] * 8, zero
        for p, a, b, det, above in pivots:
            ia = 1.0 / a
            ratio, second = b * ia, det * ia
            d = jnp.where(at[p], a, jnp.where(at[p + 1], second, d))
            ldl[p] = jnp.where(at[p], a, ldl[p])
            ldl[p + 1] = jnp.where(at[p], b, jnp.where(at[p + 1], second, ldl[p + 1]))
            for j, (s0, s1) in above.items():
                ldl[j] = jnp.where(at[p], s0, jnp.where(at[p + 1], s1 - ratio * s0, ldl[j]))
        q = lax.rsqrt(d)
        upper.append(jnp.where(lane >= 8 * r + sub, q * combine(ldl, xb), 0.0))
        lower_inv.append(q * combine(ldl, xib))
        if r < n - 1:
            k = -(-len(side_work) // (n - 1 - r))
            for work in side_work[:k]:
                work()
            side_work = side_work[k:]
    return jnp.concatenate(upper, axis=0), jnp.concatenate(lower_inv, axis=0)


def solve(early, late, a_ref, u_ref, hl_ref, lh_ref, v_ref, x_ref):
    def put(b, lo, hi, value):
        u_ref[b * NB : (b + 1) * NB, lo:hi] = value
        high, low = halves(value)
        for k, part in enumerate((high, low, high)):
            hl_ref[k * NB : (k + 1) * NB, lo:hi] = part
        if lo < K:
            e = min(hi, K)
            for k, part in enumerate((high, high, low)):
                lh_ref[k * NB : (k + 1) * NB, lo:e] = part[:, : e - lo]

    def stack(x):
        high, low = halves(x)
        return jnp.concatenate([high, low, high], axis=0)

    first_inv = K + HALF
    side_work = early
    for b in range(3):
        o, n = b * NB, (b + 1) * NB
        end = first_inv + n
        u, v = factor([a_ref[o + 8 * i : o + 8 * i + 8, o:n] for i in range(16)], side_work)
        u_ref[o:n, o:n] = u
        high, low = halves(v)
        v_ref[...] = jnp.concatenate([high, high, low], axis=1)
        put(b, n, n + NB, dot(v_ref[...], stack(a_ref[o:n, n : n + NB])))
        a_ref[n : n + NB, n : n + NB] -= dot(
            lh_ref[:, n : n + NB], hl_ref[:, n : n + NB], ((0,), (0,))
        )
        put(b, first_inv + o, end, v)

        def rest(b=b, o=o, n=n):
            lo, hi = n + NB, first_inv + o
            put(b, lo, hi, dot(v_ref[...], stack(a_ref[o:n, lo:hi])))

        def trail(r, lo, end=end):
            rows = slice(r * NB, (r + 1) * NB)
            a_ref[rows, lo:end] -= dot(lh_ref[:, rows], hl_ref[:, lo:end], ((0,), (0,)))

        def partial(o=o, n=n, end=end):
            y = u_ref[o:n, K:first_inv].astype(BF16)
            part = dot(
                hl_ref[: 2 * NB, first_inv:end], jnp.concatenate([y, y], axis=0), ((0,), (0,))
            )
            if o:
                x_ref[:o, :] += part[:o]
            x_ref[o:n, :] = part[o:]

        side_work = [rest, functools.partial(trail, b + 1, n + NB)]
        side_work += [functools.partial(trail, r, r * NB) for r in range(b + 2, 4)]
        side_work.append(partial)
    o = 3 * NB
    side_work += late
    u, v = factor([a_ref[o + 8 * i : o + 8 * i + 8, o:K] for i in range(16)], side_work)
    u_ref[o:K, o:K] = u
    high, low = halves(v)
    yw = dot(jnp.concatenate([high, high, low], axis=1), stack(a_ref[o:K, K : first_inv + o]))
    y = yw[:, :HALF].astype(BF16)
    high, low = halves(jnp.concatenate([yw[:, HALF:], v], axis=1))
    part = dot(
        jnp.concatenate([high, low], axis=0), jnp.concatenate([y, y], axis=0), ((0,), (0,))
    )
    return jnp.concatenate([x_ref[:o, :] + part[:o], part[o:]], axis=0)


def solve_body(core, pack_ref, other_ref, corr_ref, left_ref, count, late, g_ref, t_ref, a_ref,
               *scratch):
    pieces = pack_ref.shape[0]
    part, step = NG // pieces, 2 * K // pieces
    where = {ij: (c, n * NB) for c in range(2) for n, ij in enumerate(BLOCKS[c])}
    diag = lax.broadcasted_iota(jnp.int32, (NB, NB), 0) == lax.broadcasted_iota(
        jnp.int32, (NB, NB), 1
    )
    ready = set()
    root, qrow, qcol = [None] * 4, [None] * 4, [None] * 4

    def unpack(c, p):
        for i in range(p // part, (p + NB - 1) // part + 1):
            if (c, i) not in ready:
                ready.add((c, i))
                mine, theirs = pack_ref[i].astype(F32), other_ref[i].astype(F32)
                t_ref[i] = jnp.where(core == c, mine, theirs)
                q = c * NG + i * part
                g_ref[q : q + part, :] = t_ref[i, :part, :]

    def block(i, j):
        c, p = where[i, j]
        unpack(c, p)
        mean = dot(
            left_ref[:pieces, i * NB : (i + 1) * NB],
            left_ref[:pieces, j * NB : (j + 1) * NB],
            ((0,), (0,)),
        )
        return g_ref[c * NG + p : c * NG + p + NB, :] + count * mean

    def diagonal(b):
        g = block(b, b)
        only = jnp.where(diag, g, 0.0)
        row = jnp.sum(only, axis=0, keepdims=True)
        qrow[b] = lax.rsqrt(row)
        qcol[b] = lax.rsqrt(jnp.sum(only, axis=1, keepdims=True))
        root[b] = row * qrow[b]
        rows = slice(b * NB, (b + 1) * NB)
        a_ref[rows, rows] = g * qcol[b] * qrow[b]

    def off_diagonal(i, j):
        a_ref[i * NB : (i + 1) * NB, j * NB : (j + 1) * NB] = block(i, j) * qcol[i] * qrow[j]

    def right_side(b):
        rows = slice(b * NB, (b + 1) * NB)
        for h in range(2):
            for o in range(b * NB, (b + 1) * NB, step):
                i = (h * K + o) // step
                lanes = slice(K + h * NB, K + (h + 1) * NB)
                c = pack_ref[i].astype(F32)[part : part + step]
                a_ref[o : o + step, lanes] = c + corr_ref[o : o + step, h * NB : (h + 1) * NB]
        a_ref[rows, K : K + HALF] *= qcol[b]
        a_ref[rows, K + HALF :] = jnp.zeros((NB, K), F32)

    diagonal(0)
    early = [functools.partial(diagonal, b) for b in range(1, 4)]
    early += [functools.partial(off_diagonal, i, j) for i in range(4) for j in range(i + 1, 4)]
    early += [functools.partial(right_side, b) for b in range(4)]
    x = solve(early, late, a_ref, *scratch)
    rows = [(x[b * NB : (b + 1) * NB] * qcol[b]).astype(BF16) for b in range(4)]
    return jnp.concatenate(rows, axis=0), root


def block_weights(w_ref, bd_ref):
    group, width = w_ref.shape[1:]

    def write(tap):
        bi = lax.broadcasted_iota(jnp.int32, (width, width), 0)
        bj = lax.broadcasted_iota(jnp.int32, (width, width), 1)
        tiled = jnp.concatenate([w_ref[tap].astype(F32)] * (width // group), axis=0)
        same = lax.div(bi, group) == lax.div(bj, group)
        bd_ref[tap * width : (tap + 1) * width, :] = jnp.where(same, tiled, 0.0).astype(BF16)

    return [functools.partial(write, tap) for tap in range(9)]


def conv_body(core, p_ref, r_ref, keep_ref, send_ref, pad_ref, win_ref, bd_ref):
    n = r_ref.shape[0]
    width = r_ref.shape[1]
    row = lax.broadcasted_iota(jnp.int32, (n, width), 0)
    q = lax.rem(row, SIDE * SIDE)
    y, x = lax.div(q, SIDE), lax.rem(q, SIDE)
    for tap in range(9):
        a, b = tap // 3 - 1, tap % 3 - 1
        d = 8 + a * SIDE + b
        window = pad_ref[d : d + n, :]
        ok = None
        if a:
            ok = (y > 0) if a < 0 else (y < SIDE - 1)
        if b:
            okx = (x > 0) if b < 0 else (x < SIDE - 1)
            ok = okx if ok is None else ok & okx
        if ok is not None:
            window = jnp.where(ok, window, 0.0)
        win_ref[:, tap * width : (tap + 1) * width] = window.astype(BF16)
    r = dot(win_ref[...], bd_ref[...]).astype(BF16)
    r_ref[...] = r
    mine = pl.multiple_of(core * HALF, HALF)
    theirs = pl.multiple_of((1 - core) * HALF, HALF)
    send_ref[...] = dot(r, p_ref[:, pl.ds(theirs, HALF)]).astype(BF16)
    keep_ref[...] = dot(r, p_ref[:, pl.ds(mine, HALF)])


def pad_field(pad_ref, field):
    n, width = field.shape
    pad_ref[0:8, :] = jnp.zeros((8, width), F32)
    pad_ref[8 + n : 16 + n, :] = jnp.zeros((8, width), F32)
    pad_ref[8 : 8 + n, :] = field


def first_kernel(core_ref, f_hbm, w_hbm, p_hbm, r_ref, keep_ref, send_ref, pad_ref, win_ref, bd_ref,
                 f_ref, w_ref, p_ref, sems):
    copies = [
        pltpu.make_async_copy(src, dst, sems.at[k])
        for k, (src, dst) in enumerate(((w_hbm, w_ref), (f_hbm, f_ref), (p_hbm, p_ref)))
    ]
    for copy in copies:
        copy.start()
    copies[0].wait()
    for write in block_weights(w_ref, bd_ref):
        write()
    copies[1].wait()
    pad_field(pad_ref, f_ref[...].astype(F32))
    copies[2].wait()
    conv_body(core_ref[0], p_ref, r_ref, keep_ref, send_ref, pad_ref, win_ref, bd_ref)


def middle_kernel(count, core_ref, pack_ref, other_ref, corr_ref, left_ref, s_ref, w_ref, p_ref,
                  r_ref, keep_ref, send_ref, pad_ref, win_ref, bd_ref, *scratch):
    core = core_ref[0]
    late = block_weights(w_ref, bd_ref)
    mapped, _ = solve_body(
        core, pack_ref, other_ref, corr_ref, left_ref, count, late, *scratch
    )
    restored = dot(s_ref[...], mapped).astype(BF16).astype(F32)
    pad_field(pad_ref, jnp.maximum(restored, 0.0))
    conv_body(core, p_ref, r_ref, keep_ref, send_ref, pad_ref, win_ref, bd_ref)


def last_kernel(count, scale, core_ref, pack_ref, other_ref, corr_ref, left_ref, s_ref, out_ref,
                tri_ref, g_ref, t_ref, a_ref, u_ref, *scratch):
    mapped, root = solve_body(
        core_ref[0], pack_ref, other_ref, corr_ref, left_ref, count, [], g_ref, t_ref, a_ref,
        u_ref, *scratch,
    )
    out_ref[...] = dot(s_ref[...], mapped).astype(BF16)
    for b in range(4):
        lanes = slice(b * NB, (b + 1) * NB)
        rows = (b + 1) * NB
        tri_ref[:rows, lanes] = u_ref[:rows, lanes] * (root[b] * scale)
        if rows < K:
            tri_ref[rows:, lanes] = jnp.zeros((K - rows, NB), F32)


def gram_kernel(core_ref, own_ref, other_ref, r_ref, s_ref, m_ref, g_ref, t_ref):
    core = core_ref[0]
    n = own_ref.shape[0]
    pieces = t_ref.shape[0]
    s_ref[:, pl.ds(pl.multiple_of(core * HALF, HALF), HALF)] = own_ref[...]
    s_ref[:, pl.ds(pl.multiple_of((1 - core) * HALF, HALF), HALF)] = other_ref[...]
    s, r = s_ref[...], r_ref[...]
    ones = jnp.ones((8, n), BF16)
    mean = (dot(ones, s) * (1.0 / n)).astype(BF16).astype(F32)
    total = dot(ones, r)
    high = total.astype(BF16).astype(F32)
    low = (total - high).astype(BF16).astype(F32)
    first = lax.broadcasted_iota(jnp.int32, (8, K), 0) < 1
    left = jnp.where(lax.broadcasted_iota(jnp.int32, (8, K), 0) < 2, mean, 0.0).astype(BF16)
    only = jnp.where(first, mean, 0.0).astype(BF16)
    right = jnp.where(first[:, :HALF], high, low).astype(BF16)
    cross = dot(s, r, ((0,), (0,))) - dot(left, right, ((0,), (0,)))
    extra = jnp.concatenate(
        [mean[:1, h * NB : (h + 1) * NB] for h in range(4)]
        + [high[:1, h * NB : (h + 1) * NB] for h in range(2)]
        + [low[:1, h * NB : (h + 1) * NB] for h in range(2)],
        axis=0,
    )
    for c in range(2):

        @pl.when(core == c)
        def _():
            for k, (i, j) in enumerate(BLOCKS[c]):
                a, b = slice(i * NB, (i + 1) * NB), slice(j * NB, (j + 1) * NB)
                block = dot(s_ref[:, a], s_ref[:, b], ((0,), (0,)))
                g_ref[k * NB : (k + 1) * NB, :] = block - n * dot(
                    only[:, a], only[:, b], ((0,), (0,))
                )

    part = NG // pieces
    step = 2 * K // pieces
    for i in range(pieces):
        t_ref[i, :part, :] = g_ref[i * part : (i + 1) * part, :]
        h, o = divmod(i * step, K)
        t_ref[i, part : part + step, :] = cross[o : o + step, h * NB : (h + 1) * NB]
        t_ref[i, part + step : part + step + 8, :] = extra
        t_ref[i, part + step + 8 :, :] = jnp.zeros((SEND - part - step - 8, NB), F32)
    m_ref[...] = t_ref[...].astype(BF16)


def sum_kernel(core_ref, parts_ref, out_ref, corr_ref, left_ref, l_ref, right_ref):
    pieces = parts_ref.shape[0]
    part, step = NG // pieces, 2 * K // pieces
    acc = None
    for i in range(pieces):
        piece = parts_ref[i].astype(F32)
        acc = piece if acc is None else acc + piece
        e = piece[part + step : part + step + 8]
        for k in range(2):
            q = pieces * k + i
            for h in range(4):
                l_ref[q : q + 1, h * NB : (h + 1) * NB] = e[h : h + 1]
            for h in range(2):
                right_ref[q : q + 1, h * NB : (h + 1) * NB] = e[4 + 2 * k + h : 5 + 2 * k + h]
    total = acc[:RETURN].astype(BF16)
    for i in range(pieces):
        out_ref[i] = total
    left = l_ref[...].astype(BF16)
    left_ref[...] = left
    corr_ref[...] = dot(left, right_ref[...].astype(BF16), ((0,), (0,)))


def fold_kernel(core_ref, parts_ref, out_ref):
    acc = parts_ref[0].astype(F32)
    for i in range(1, parts_ref.shape[0]):
        acc = acc + parts_ref[i].astype(F32)
    out_ref[...] = acc.astype(BF16)


def solve_scratch(pieces):
    total = 2 * K + HALF
    return [
        pltpu.VMEM((2 * NG, NB), F32),
        pltpu.VMEM((pieces, RETURN, NB), F32),
        pltpu.VMEM((K, total), F32),
        pltpu.VMEM((K, total), F32),
        pltpu.VMEM((3 * NB, total), BF16),
        pltpu.VMEM((3 * NB, K), BF16),
        pltpu.VMEM((NB, 3 * NB), BF16),
        pltpu.VMEM((K, HALF), F32),
    ]


def conv_scratch(n, width):
    return [
        pltpu.VMEM((n + 16, width), F32),
        pltpu.VMEM((n, 9 * width), BF16),
        pltpu.VMEM((9 * width, width), BF16),
    ]


def conv_outs(n, width):
    return (
        jax.ShapeDtypeStruct((n, width), BF16),
        jax.ShapeDtypeStruct((n, HALF), F32),
        jax.ShapeDtypeStruct((n, HALF), BF16),
    )


def call(kernel, name, outs, args, scratch=(), space=VMEM):
    return pl.pallas_call(
        kernel,
        out_shape=outs,
        in_specs=[SMEM] + [space] * (len(args) - 1),
        out_specs=jax.tree.map(lambda _: VMEM, outs),
        scratch_shapes=list(scratch),
        compiler_params=PARAMS,
        name=name,
    )(*args)


SWAP = ((0, 1), (1, 0))
ROWS = ("z", "y")


def spread(x, axes):
    n = lax.axis_size(axes)
    return lax.all_to_all(jnp.broadcast_to(x[None], (n,) + x.shape), axes, 0, 0)


def sketch_of(core, keep, send):
    pair = (keep + lax.ppermute(send, "core", SWAP).astype(F32)).astype(BF16)
    own = call(
        fold_kernel, "fold", jax.ShapeDtypeStruct(pair.shape, BF16), (core, spread(pair, "x"))
    )
    return own, lax.ppermute(own, "core", SWAP)


def compress_sums(core, r, keep, send):
    own, other = sketch_of(core, keep, send)
    n = r.shape[0]
    pieces = lax.axis_size(ROWS)
    outs = (
        jax.ShapeDtypeStruct((n, K), BF16),
        jax.ShapeDtypeStruct((pieces, SEND, NB), BF16),
    )
    scratch = [pltpu.VMEM((NG, NB), F32), pltpu.VMEM((pieces, SEND, NB), F32)]
    s, m = call(gram_kernel, "gram", outs, (core, own, other, r), scratch)
    parts = lax.all_to_all(m, ROWS, 0, 0)
    outs = (
        jax.ShapeDtypeStruct((pieces, RETURN, NB), BF16),
        jax.ShapeDtypeStruct((K, HALF), F32),
        jax.ShapeDtypeStruct((2 * pieces, K), BF16),
    )
    scratch = [pltpu.VMEM((2 * pieces, K), F32), pltpu.VMEM((2 * pieces, HALF), F32)]
    total, corr, left = call(sum_kernel, "sum", outs, (core, parts), scratch)
    pack = lax.all_to_all(total, ROWS, 0, 0)
    return pack, lax.ppermute(pack, "core", SWAP), corr, left, s


def per_device(inputs, conv_one, conv_two, probe_one, probe_two):
    n, width = inputs.shape
    pieces = lax.axis_size(ROWS)
    total_rows = n * pieces
    core = lax.axis_index("core").astype(jnp.int32).reshape(1)
    outs = conv_outs(n, width)
    args = (inputs, conv_one, probe_one)
    scratch = conv_scratch(n, width) + [pltpu.VMEM(x.shape, x.dtype) for x in args]
    scratch.append(pltpu.SemaphoreType.DMA((len(args),)))
    pinned = [pltpu.with_memory_space_constraint(x, pltpu.HBM) for x in args]
    r, keep, send = call(first_kernel, "first", outs, (core, *pinned), scratch, HBM)
    sums = compress_sums(core, r, keep, send)
    r, keep, send = call(
        functools.partial(middle_kernel, n), "middle", outs, (core, *sums, conv_two, probe_two),
        conv_scratch(n, width) + solve_scratch(pieces),
    )
    sums = compress_sums(core, r, keep, send)
    outs = (jax.ShapeDtypeStruct((n, width), BF16), jax.ShapeDtypeStruct((K, K), F32))
    return call(
        functools.partial(last_kernel, n, 1.0 / math.sqrt(total_rows)), "last", outs, (core, *sums),
        solve_scratch(pieces),
    )


def solution(mesh):
    grid = Mesh(mesh.devices.reshape(8, 4, 4, 2), ("z", "y", "x", "core"))
    rows, chan = ("z", "y"), ("x", "core")
    in_specs = (
        P(rows, chan),
        P(None, None, chan),
        P(None, None, chan),
        P(chan, None),
        P(chan, None),
    )
    out_specs = (P(rows, chan), P())
    return jax.shard_map(
        per_device, mesh=grid, in_specs=in_specs, out_specs=out_specs, check_vma=False
    )
```

```python
import functools
import math

import jax
import jax.numpy as jnp
from jax import lax
from jax.experimental import pallas as pl
from jax.experimental.pallas import tpu as pltpu
from jax.sharding import Mesh, PartitionSpec as P

SIDE = 7
K = 512
NB = 128
HALF = 256
F32 = jnp.float32
BF16 = jnp.bfloat16
VMEM = pl.BlockSpec(memory_space=pltpu.VMEM)
SMEM = pl.BlockSpec(memory_space=pltpu.SMEM)
HBM = pl.BlockSpec(memory_space=pltpu.HBM)
PARAMS = pltpu.CompilerParams(vmem_limit_bytes=48 << 20)
BLOCKS = (((0, 0), (0, 1), (0, 2), (0, 3), (1, 1)), ((1, 2), (1, 3), (2, 2), (2, 3), (3, 3)))
NG = 5 * NB
PIECE = 56


def dot(a, b, dims=((1,), (0,))):
    return lax.dot_general(a, b, (dims, ((), ())), preferred_element_type=F32)


def bcast_lane(x, k):
    return jnp.broadcast_to(x[:, k : k + 1], (8, NB))


def bcast_row(x, k):
    return jnp.broadcast_to(x[k : k + 1, :], (8, NB))


def combine(coeffs, rows):
    p = [c * b for c, b in zip(coeffs, rows)]
    while len(p) > 1:
        p = [p[i] + p[i + 1] for i in range(0, len(p), 2)]
    return p[0]


def halves(x):
    high = x.astype(BF16)
    return high, (x - high.astype(F32)).astype(BF16)


def factor(rows, side_work):
    n = len(rows)
    sub = lax.broadcasted_iota(jnp.int32, (8, NB), 0)
    lane = lax.broadcasted_iota(jnp.int32, (8, NB), 1)
    at = [sub == i for i in range(8)]
    zero = jnp.zeros((8, NB), F32)
    unit = [(sub == i).astype(F32) for i in range(8)]
    inv = [(lane == sub + 8 * r).astype(F32) for r in range(n)]
    rows, side_work = list(rows), list(side_work)
    upper, lower_inv = [], []
    for r in range(n):
        top, top_inv = rows[r], inv[r]
        cols = [bcast_lane(top, 8 * r + k) for k in range(8)]
        rb = [bcast_row(top, j) for j in range(8)]
        ib = [bcast_row(top_inv, j) for j in range(8)]
        pivots = []
        for p in range(0, 8, 2):
            a, b, c = bcast_row(cols[p], p), bcast_row(cols[p], p + 1), bcast_row(cols[p + 1], p + 1)
            det = a * c - b * b
            idet = 1.0 / det
            w0 = cols[p] * c - cols[p + 1] * b
            w1 = cols[p + 1] * a - cols[p] * b
            w0 = jnp.where(at[p], det - c, jnp.where(at[p + 1], b, w0))
            w1 = jnp.where(at[p], b, jnp.where(at[p + 1], det - a, w1))
            z0, z1 = w0 * idet, w1 * idet
            new, above = list(cols), {}
            for j in range(8):
                if j in (p, p + 1):
                    continue
                s0, s1 = bcast_row(cols[j], p), bcast_row(cols[j], p + 1)
                if j in (p + 2, p + 3):
                    new[j] = cols[j] - (w0 * s0 + w1 * s1) * idet
                else:
                    new[j] = cols[j] - (z0 * s0 + z1 * s1)
                if j > p:
                    above[j] = (s0, s1)
            new[p], new[p + 1] = unit[p] - z0, unit[p + 1] - z1
            pivots.append((p, a, b, det, above))
            cols = new
        x, xi = combine(cols, rb), combine(cols, ib)
        xb = [bcast_row(x, k) for k in range(8)]
        xib = [bcast_row(xi, k) for k in range(8)]
        for g in range(r + 1, n):
            cg = [bcast_lane(rows[g], 8 * r + k) for k in range(8)]
            rows[g], inv[g] = rows[g] - combine(cg, xb), inv[g] - combine(cg, xib)
        ldl, d = [zero] * 8, zero
        for p, a, b, det, above in pivots:
            ia = 1.0 / a
            ratio, second = b * ia, det * ia
            d = jnp.where(at[p], a, jnp.where(at[p + 1], second, d))
            ldl[p] = jnp.where(at[p], a, ldl[p])
            ldl[p + 1] = jnp.where(at[p], b, jnp.where(at[p + 1], second, ldl[p + 1]))
            for j, (s0, s1) in above.items():
                ldl[j] = jnp.where(at[p], s0, jnp.where(at[p + 1], s1 - ratio * s0, ldl[j]))
        q = lax.rsqrt(d)
        upper.append(jnp.where(lane >= 8 * r + sub, q * combine(ldl, xb), 0.0))
        lower_inv.append(q * combine(ldl, xib))
        if r < n - 1:
            k = -(-len(side_work) // (n - 1 - r))
            for work in side_work[:k]:
                work()
            side_work = side_work[k:]
    return jnp.concatenate(upper, axis=0), jnp.concatenate(lower_inv, axis=0)


def solve(early, late, a_ref, u_ref, hl_ref, lh_ref, v_ref, x_ref):
    def put(b, lo, hi, value):
        u_ref[b * NB : (b + 1) * NB, lo:hi] = value
        high, low = halves(value)
        for k, part in enumerate((high, low, high)):
            hl_ref[k * NB : (k + 1) * NB, lo:hi] = part
        if lo < K:
            e = min(hi, K)
            for k, part in enumerate((high, high, low)):
                lh_ref[k * NB : (k + 1) * NB, lo:e] = part[:, : e - lo]

    def stack(x):
        high, low = halves(x)
        return jnp.concatenate([high, low, high], axis=0)

    first_inv = K + HALF
    side_work = early
    for b in range(3):
        o, n = b * NB, (b + 1) * NB
        end = first_inv + n
        u, v = factor([a_ref[o + 8 * i : o + 8 * i + 8, o:n] for i in range(16)], side_work)
        u_ref[o:n, o:n] = u
        high, low = halves(v)
        v_ref[...] = jnp.concatenate([high, high, low], axis=1)
        put(b, n, n + NB, dot(v_ref[...], stack(a_ref[o:n, n : n + NB])))
        a_ref[n : n + NB, n : n + NB] -= dot(
            lh_ref[:, n : n + NB], hl_ref[:, n : n + NB], ((0,), (0,))
        )
        put(b, first_inv + o, end, v)

        def rest(b=b, o=o, n=n):
            lo, hi = n + NB, first_inv + o
            put(b, lo, hi, dot(v_ref[...], stack(a_ref[o:n, lo:hi])))

        def trail(r, lo, end=end):
            rows = slice(r * NB, (r + 1) * NB)
            a_ref[rows, lo:end] -= dot(lh_ref[:, rows], hl_ref[:, lo:end], ((0,), (0,)))

        def partial(o=o, n=n, end=end):
            y = u_ref[o:n, K:first_inv].astype(BF16)
            part = dot(
                hl_ref[: 2 * NB, first_inv:end], jnp.concatenate([y, y], axis=0), ((0,), (0,))
            )
            if o:
                x_ref[:o, :] += part[:o]
            x_ref[o:n, :] = part[o:]

        side_work = [rest, functools.partial(trail, b + 1, n + NB)]
        side_work += [functools.partial(trail, r, r * NB) for r in range(b + 2, 4)]
        side_work.append(partial)
    o = 3 * NB
    side_work += late
    u, v = factor([a_ref[o + 8 * i : o + 8 * i + 8, o:K] for i in range(16)], side_work)
    u_ref[o:K, o:K] = u
    high, low = halves(v)
    yw = dot(jnp.concatenate([high, high, low], axis=1), stack(a_ref[o:K, K : first_inv + o]))
    y = yw[:, :HALF].astype(BF16)
    high, low = halves(jnp.concatenate([yw[:, HALF:], v], axis=1))
    part = dot(
        jnp.concatenate([high, low], axis=0), jnp.concatenate([y, y], axis=0), ((0,), (0,))
    )
    return jnp.concatenate([x_ref[:o, :] + part[:o], part[o:]], axis=0)


def solve_body(core, pack_ref, other_ref, left_ref, count, late, right_ref, g_ref, t_ref, a_ref,
               *scratch):
    pieces = pack_ref.shape[0]
    part, step = NG // pieces, 2 * K // pieces
    where = {ij: (c, n * NB) for c in range(2) for n, ij in enumerate(BLOCKS[c])}
    diag = lax.broadcasted_iota(jnp.int32, (NB, NB), 0) == lax.broadcasted_iota(
        jnp.int32, (NB, NB), 1
    )
    ready = set()
    root, qrow, qcol = [None] * 4, [None] * 4, [None] * 4

    def unpack(c, p):
        for i in range(p // part, (p + NB - 1) // part + 1):
            if (c, i) not in ready:
                ready.add((c, i))
                mine, theirs = pack_ref[i].astype(F32), other_ref[i].astype(F32)
                t_ref[i] = jnp.where(core == c, mine, theirs)
                q = c * NG + i * part
                g_ref[q : q + part, :] = t_ref[i, :part, :]

    def block(i, j):
        c, p = where[i, j]
        unpack(c, p)
        mean = dot(
            left_ref[:pieces, i * NB : (i + 1) * NB],
            left_ref[:pieces, j * NB : (j + 1) * NB],
            ((0,), (0,)),
        )
        return g_ref[c * NG + p : c * NG + p + NB, :] + count * mean

    def diagonal(b):
        g = block(b, b)
        only = jnp.where(diag, g, 0.0)
        row = jnp.sum(only, axis=0, keepdims=True)
        qrow[b] = lax.rsqrt(row)
        qcol[b] = lax.rsqrt(jnp.sum(only, axis=1, keepdims=True))
        root[b] = row * qrow[b]
        rows = slice(b * NB, (b + 1) * NB)
        a_ref[rows, rows] = g * qcol[b] * qrow[b]

    def off_diagonal(i, j):
        a_ref[i * NB : (i + 1) * NB, j * NB : (j + 1) * NB] = block(i, j) * qcol[i] * qrow[j]

    def sums():
        for i in range(pieces):
            e = pack_ref[i].astype(F32)[part + step :]
            for k in range(2):
                for h in range(2):
                    q = pieces * k + i
                    right_ref[q : q + 1, h * NB : (h + 1) * NB] = e[2 * k + h : 2 * k + h + 1]

    def right_side(b):
        rows = slice(b * NB, (b + 1) * NB)
        mean = dot(left_ref[:, rows], right_ref[...].astype(BF16), ((0,), (0,)))
        for h in range(2):
            for o in range(b * NB, (b + 1) * NB, step):
                i = (h * K + o) // step
                lanes = slice(K + h * NB, K + (h + 1) * NB)
                c = pack_ref[i].astype(F32)[part : part + step]
                q = o - b * NB
                a_ref[o : o + step, lanes] = c + mean[q : q + step, h * NB : (h + 1) * NB]
        a_ref[rows, K : K + HALF] *= qcol[b]
        a_ref[rows, K + HALF :] = jnp.zeros((NB, K), F32)

    diagonal(0)
    early = [functools.partial(diagonal, b) for b in range(1, 4)]
    early += [functools.partial(off_diagonal, i, j) for i in range(4) for j in range(i + 1, 4)]
    early += [sums] + [functools.partial(right_side, b) for b in range(4)]
    x = solve(early, late, a_ref, *scratch)
    rows = [(x[b * NB : (b + 1) * NB] * qcol[b]).astype(BF16) for b in range(4)]
    return jnp.concatenate(rows, axis=0), root


def block_weights(w_ref, bd_ref):
    group, width = w_ref.shape[1:]

    def write(tap):
        bi = lax.broadcasted_iota(jnp.int32, (width, width), 0)
        bj = lax.broadcasted_iota(jnp.int32, (width, width), 1)
        tiled = jnp.concatenate([w_ref[tap].astype(F32)] * (width // group), axis=0)
        same = lax.div(bi, group) == lax.div(bj, group)
        bd_ref[tap * width : (tap + 1) * width, :] = jnp.where(same, tiled, 0.0).astype(BF16)

    return [functools.partial(write, tap) for tap in range(9)]


def conv_body(core, p_ref, r_ref, keep_ref, send_ref, pad_ref, win_ref, bd_ref):
    n = r_ref.shape[0]
    width = r_ref.shape[1]
    row = lax.broadcasted_iota(jnp.int32, (n, width), 0)
    q = lax.rem(row, SIDE * SIDE)
    y, x = lax.div(q, SIDE), lax.rem(q, SIDE)
    for tap in range(9):
        a, b = tap // 3 - 1, tap % 3 - 1
        d = 8 + a * SIDE + b
        window = pad_ref[d : d + n, :]
        ok = None
        if a:
            ok = (y > 0) if a < 0 else (y < SIDE - 1)
        if b:
            okx = (x > 0) if b < 0 else (x < SIDE - 1)
            ok = okx if ok is None else ok & okx
        if ok is not None:
            window = jnp.where(ok, window, 0.0)
        win_ref[:, tap * width : (tap + 1) * width] = window.astype(BF16)
    r = dot(win_ref[...], bd_ref[...]).astype(BF16)
    r_ref[...] = r
    mine = pl.multiple_of(core * HALF, HALF)
    theirs = pl.multiple_of((1 - core) * HALF, HALF)
    send_ref[...] = dot(r, p_ref[:, pl.ds(theirs, HALF)]).astype(BF16)
    keep_ref[...] = dot(r, p_ref[:, pl.ds(mine, HALF)])


def pad_field(pad_ref, field):
    n, width = field.shape
    pad_ref[0:8, :] = jnp.zeros((8, width), F32)
    pad_ref[8 + n : 16 + n, :] = jnp.zeros((8, width), F32)
    pad_ref[8 : 8 + n, :] = field


def first_kernel(core_ref, f_hbm, w_hbm, p_hbm, r_ref, keep_ref, send_ref, pad_ref, win_ref, bd_ref,
                 f_ref, w_ref, p_ref, sems):
    copies = [
        pltpu.make_async_copy(src, dst, sems.at[k])
        for k, (src, dst) in enumerate(((w_hbm, w_ref), (f_hbm, f_ref), (p_hbm, p_ref)))
    ]
    for copy in copies:
        copy.start()
    copies[0].wait()
    for write in block_weights(w_ref, bd_ref):
        write()
    copies[1].wait()
    pad_field(pad_ref, f_ref[...].astype(F32))
    copies[2].wait()
    conv_body(core_ref[0], p_ref, r_ref, keep_ref, send_ref, pad_ref, win_ref, bd_ref)


def middle_kernel(count, core_ref, pack_ref, other_ref, left_ref, s_ref, w_ref, p_ref,
                  r_ref, keep_ref, send_ref, pad_ref, win_ref, bd_ref, *scratch):
    core = core_ref[0]
    late = block_weights(w_ref, bd_ref)
    mapped, _ = solve_body(core, pack_ref, other_ref, left_ref, count, late, *scratch)
    restored = dot(s_ref[...], mapped).astype(BF16).astype(F32)
    pad_field(pad_ref, jnp.maximum(restored, 0.0))
    conv_body(core, p_ref, r_ref, keep_ref, send_ref, pad_ref, win_ref, bd_ref)


def last_kernel(count, scale, core_ref, pack_ref, other_ref, left_ref, s_ref, out_ref, tri_ref,
                right_ref, g_ref, t_ref, a_ref, u_ref, *scratch):
    mapped, root = solve_body(
        core_ref[0], pack_ref, other_ref, left_ref, count, [], right_ref, g_ref, t_ref, a_ref,
        u_ref, *scratch,
    )
    out_ref[...] = dot(s_ref[...], mapped).astype(BF16)
    for b in range(4):
        lanes = slice(b * NB, (b + 1) * NB)
        rows = (b + 1) * NB
        tri_ref[:rows, lanes] = u_ref[:rows, lanes] * (root[b] * scale)
        if rows < K:
            tri_ref[rows:, lanes] = jnp.zeros((K - rows, NB), F32)


def gram_kernel(core_ref, own_ref, other_ref, r_ref, s_ref, m_ref, sums_ref, g_ref, t_ref):
    core = core_ref[0]
    n = own_ref.shape[0]
    pieces = t_ref.shape[0]
    s_ref[:, pl.ds(pl.multiple_of(core * HALF, HALF), HALF)] = own_ref[...]
    s_ref[:, pl.ds(pl.multiple_of((1 - core) * HALF, HALF), HALF)] = other_ref[...]
    s, r = s_ref[...], r_ref[...]
    ones = jnp.ones((8, n), BF16)
    mean = (dot(ones, s) * (1.0 / n)).astype(BF16).astype(F32)
    total = dot(ones, r)
    high = total.astype(BF16).astype(F32)
    low = (total - high).astype(BF16).astype(F32)
    first = lax.broadcasted_iota(jnp.int32, (8, K), 0) < 1
    left = jnp.where(lax.broadcasted_iota(jnp.int32, (8, K), 0) < 2, mean, 0.0).astype(BF16)
    only = jnp.where(first, mean, 0.0).astype(BF16)
    right = jnp.where(first[:, :HALF], high, low).astype(BF16)
    cross = dot(s, r, ((0,), (0,))) - dot(left, right, ((0,), (0,)))
    extra = jnp.concatenate([mean[:1, h * NB : (h + 1) * NB] for h in range(4)], axis=0)
    sums = [x[:1, h * NB : (h + 1) * NB] for x in (high, low) for h in range(2)]
    sums_ref[...] = jnp.concatenate(sums + sums, axis=0)
    for c in range(2):

        @pl.when(core == c)
        def _():
            for k, (i, j) in enumerate(BLOCKS[c]):
                a, b = slice(i * NB, (i + 1) * NB), slice(j * NB, (j + 1) * NB)
                block = dot(s_ref[:, a], s_ref[:, b], ((0,), (0,)))
                g_ref[k * NB : (k + 1) * NB, :] = block - n * dot(
                    only[:, a], only[:, b], ((0,), (0,))
                )

    part = NG // pieces
    step = 2 * K // pieces
    for i in range(pieces):
        t_ref[i, :part, :] = g_ref[i * part : (i + 1) * part, :]
        h, o = divmod(i * step, K)
        t_ref[i, part : part + step, :] = cross[o : o + step, h * NB : (h + 1) * NB]
        t_ref[i, part + step :, :] = extra
    m_ref[...] = t_ref[...].astype(BF16)


def sum_kernel(core_ref, parts_ref, sums_ref, out_ref, left_ref, l_ref):
    pieces = parts_ref.shape[0]
    used = (NG + 2 * K) // pieces
    acc = None
    for i in range(pieces):
        piece = parts_ref[i].astype(F32)
        acc = piece if acc is None else acc + piece
        for h in range(4):
            mean = piece[used + h : used + h + 1]
            for k in range(2):
                q = pieces * k + i
                l_ref[q : q + 1, h * NB : (h + 1) * NB] = mean
    total = jnp.concatenate([acc[:used], sums_ref[: PIECE - used, :]], axis=0).astype(BF16)
    for i in range(pieces):
        out_ref[i] = total
    left_ref[...] = l_ref[...].astype(BF16)


def fold_kernel(core_ref, parts_ref, out_ref):
    acc = parts_ref[0].astype(F32)
    for i in range(1, parts_ref.shape[0]):
        acc = acc + parts_ref[i].astype(F32)
    out_ref[...] = acc.astype(BF16)


def solve_scratch(pieces):
    total = 2 * K + HALF
    return [
        pltpu.VMEM((2 * pieces, HALF), F32),
        pltpu.VMEM((2 * NG, NB), F32),
        pltpu.VMEM((pieces, PIECE, NB), F32),
        pltpu.VMEM((K, total), F32),
        pltpu.VMEM((K, total), F32),
        pltpu.VMEM((3 * NB, total), BF16),
        pltpu.VMEM((3 * NB, K), BF16),
        pltpu.VMEM((NB, 3 * NB), BF16),
        pltpu.VMEM((K, HALF), F32),
    ]


def conv_scratch(n, width):
    return [
        pltpu.VMEM((n + 16, width), F32),
        pltpu.VMEM((n, 9 * width), BF16),
        pltpu.VMEM((9 * width, width), BF16),
    ]


def conv_outs(n, width):
    return (
        jax.ShapeDtypeStruct((n, width), BF16),
        jax.ShapeDtypeStruct((n, HALF), F32),
        jax.ShapeDtypeStruct((n, HALF), BF16),
    )


def call(kernel, name, outs, args, scratch=(), space=VMEM):
    return pl.pallas_call(
        kernel,
        out_shape=outs,
        in_specs=[SMEM] + [space] * (len(args) - 1),
        out_specs=jax.tree.map(lambda _: VMEM, outs),
        scratch_shapes=list(scratch),
        compiler_params=PARAMS,
        name=name,
    )(*args)


SWAP = ((0, 1), (1, 0))
ROWS = ("z", "y")


def spread(x, axes):
    n = lax.axis_size(axes)
    return lax.all_to_all(jnp.broadcast_to(x[None], (n,) + x.shape), axes, 0, 0)


def sketch_of(core, keep, send):
    pair = (keep + lax.ppermute(send, "core", SWAP).astype(F32)).astype(BF16)
    own = call(
        fold_kernel, "fold", jax.ShapeDtypeStruct(pair.shape, BF16), (core, spread(pair, "x"))
    )
    return own, lax.ppermute(own, "core", SWAP)


def compress_sums(core, r, keep, send):
    own, other = sketch_of(core, keep, send)
    n = r.shape[0]
    pieces = lax.axis_size(ROWS)
    outs = (
        jax.ShapeDtypeStruct((n, K), BF16),
        jax.ShapeDtypeStruct((pieces, PIECE, NB), BF16),
        jax.ShapeDtypeStruct((8, NB), F32),
    )
    scratch = [pltpu.VMEM((NG, NB), F32), pltpu.VMEM((pieces, PIECE, NB), F32)]
    s, m, sums = call(gram_kernel, "gram", outs, (core, own, other, r), scratch)
    parts = lax.all_to_all(m, ROWS, 0, 0)
    outs = (
        jax.ShapeDtypeStruct((pieces, PIECE, NB), BF16),
        jax.ShapeDtypeStruct((2 * pieces, K), BF16),
    )
    scratch = [pltpu.VMEM((2 * pieces, K), F32)]
    total, left = call(sum_kernel, "sum", outs, (core, parts, sums), scratch)
    pack = lax.all_to_all(total, ROWS, 0, 0)
    return pack, lax.ppermute(pack, "core", SWAP), left, s


def per_device(inputs, conv_one, conv_two, probe_one, probe_two):
    n, width = inputs.shape
    pieces = lax.axis_size(ROWS)
    total_rows = n * pieces
    core = lax.axis_index("core").astype(jnp.int32).reshape(1)
    outs = conv_outs(n, width)
    args = (inputs, conv_one, probe_one)
    scratch = conv_scratch(n, width) + [pltpu.VMEM(x.shape, x.dtype) for x in args]
    scratch.append(pltpu.SemaphoreType.DMA((len(args),)))
    pinned = [pltpu.with_memory_space_constraint(x, pltpu.HBM) for x in args]
    r, keep, send = call(first_kernel, "first", outs, (core, *pinned), scratch, HBM)
    sums = compress_sums(core, r, keep, send)
    r, keep, send = call(
        functools.partial(middle_kernel, n), "middle", outs, (core, *sums, conv_two, probe_two),
        conv_scratch(n, width) + solve_scratch(pieces),
    )
    sums = compress_sums(core, r, keep, send)
    outs = (jax.ShapeDtypeStruct((n, width), BF16), jax.ShapeDtypeStruct((K, K), F32))
    return call(
        functools.partial(last_kernel, n, 1.0 / math.sqrt(total_rows)), "last", outs, (core, *sums),
        solve_scratch(pieces),
    )


def solution(mesh):
    grid = Mesh(mesh.devices.reshape(8, 4, 4, 2), ("z", "y", "x", "core"))
    rows, chan = ("z", "y"), ("x", "core")
    in_specs = (
        P(rows, chan),
        P(None, None, chan),
        P(None, None, chan),
        P(chan, None),
        P(chan, None),
    )
    out_specs = (P(rows, chan), P())
    return jax.shard_map(
        per_device, mesh=grid, in_specs=in_specs, out_specs=out_specs, check_vma=False
    )
```

```python
import functools
import math

import jax
import jax.numpy as jnp
from jax import lax
from jax.experimental import pallas as pl
from jax.experimental.pallas import tpu as pltpu
from jax.sharding import Mesh, PartitionSpec as P

SIDE = 7
K = 512
NB = 128
HALF = 256
F32 = jnp.float32
BF16 = jnp.bfloat16
VMEM = pl.BlockSpec(memory_space=pltpu.VMEM)
SMEM = pl.BlockSpec(memory_space=pltpu.SMEM)
HBM = pl.BlockSpec(memory_space=pltpu.HBM)
PARAMS = pltpu.CompilerParams(vmem_limit_bytes=48 << 20)
BLOCKS = (((0, 0), (0, 1), (0, 2), (0, 3), (1, 1)), ((1, 2), (1, 3), (2, 2), (2, 3), (3, 3)))
NG = 5 * NB
PIECE = 56


def dot(a, b, dims=((1,), (0,))):
    return lax.dot_general(a, b, (dims, ((), ())), preferred_element_type=F32)


def bcast_lane(x, k):
    return jnp.broadcast_to(x[:, k : k + 1], (8, NB))


def bcast_row(x, k):
    return jnp.broadcast_to(x[k : k + 1, :], (8, NB))


def combine(coeffs, rows):
    p = [c * b for c, b in zip(coeffs, rows)]
    while len(p) > 1:
        p = [p[i] + p[i + 1] for i in range(0, len(p), 2)]
    return p[0]


def halves(x):
    high = x.astype(BF16)
    return high, (x - high.astype(F32)).astype(BF16)


def factor(rows, side_work):
    n = len(rows)
    sub = lax.broadcasted_iota(jnp.int32, (8, NB), 0)
    lane = lax.broadcasted_iota(jnp.int32, (8, NB), 1)
    at = [sub == i for i in range(8)]
    zero = jnp.zeros((8, NB), F32)
    unit = [(sub == i).astype(F32) for i in range(8)]
    inv = [(lane == sub + 8 * r).astype(F32) for r in range(n)]
    rows, side_work = list(rows), list(side_work)
    upper, lower_inv = [], []
    for r in range(n):
        top, top_inv = rows[r], inv[r]
        cols = [bcast_lane(top, 8 * r + k) for k in range(8)]
        rb = [bcast_row(top, j) for j in range(8)]
        ib = [bcast_row(top_inv, j) for j in range(8)]
        pivots = []
        for p in range(0, 8, 2):
            a, b, c = bcast_row(cols[p], p), bcast_row(cols[p], p + 1), bcast_row(cols[p + 1], p + 1)
            det = a * c - b * b
            idet = 1.0 / det
            w0 = cols[p] * c - cols[p + 1] * b
            w1 = cols[p + 1] * a - cols[p] * b
            w0 = jnp.where(at[p], det - c, jnp.where(at[p + 1], b, w0))
            w1 = jnp.where(at[p], b, jnp.where(at[p + 1], det - a, w1))
            z0, z1 = w0 * idet, w1 * idet
            new, above = list(cols), {}
            for j in range(8):
                if j in (p, p + 1):
                    continue
                s0, s1 = bcast_row(cols[j], p), bcast_row(cols[j], p + 1)
                if j in (p + 2, p + 3):
                    new[j] = cols[j] - (w0 * s0 + w1 * s1) * idet
                else:
                    new[j] = cols[j] - (z0 * s0 + z1 * s1)
                if j > p:
                    above[j] = (s0, s1)
            new[p], new[p + 1] = unit[p] - z0, unit[p + 1] - z1
            pivots.append((p, a, b, det, above))
            cols = new
        x, xi = combine(cols, rb), combine(cols, ib)
        xb = [bcast_row(x, k) for k in range(8)]
        xib = [bcast_row(xi, k) for k in range(8)]
        for g in range(r + 1, n):
            cg = [bcast_lane(rows[g], 8 * r + k) for k in range(8)]
            rows[g], inv[g] = rows[g] - combine(cg, xb), inv[g] - combine(cg, xib)
        ldl, d = [zero] * 8, zero
        for p, a, b, det, above in pivots:
            ia = 1.0 / a
            ratio, second = b * ia, det * ia
            d = jnp.where(at[p], a, jnp.where(at[p + 1], second, d))
            ldl[p] = jnp.where(at[p], a, ldl[p])
            ldl[p + 1] = jnp.where(at[p], b, jnp.where(at[p + 1], second, ldl[p + 1]))
            for j, (s0, s1) in above.items():
                ldl[j] = jnp.where(at[p], s0, jnp.where(at[p + 1], s1 - ratio * s0, ldl[j]))
        q = lax.rsqrt(d)
        upper.append(jnp.where(lane >= 8 * r + sub, q * combine(ldl, xb), 0.0))
        lower_inv.append(q * combine(ldl, xib))
        if r < n - 1:
            k = -(-len(side_work) // (n - 1 - r))
            for work in side_work[:k]:
                work()
            side_work = side_work[k:]
    return jnp.concatenate(upper, axis=0), jnp.concatenate(lower_inv, axis=0)


def solve(early, late, a_ref, u_ref, hl_ref, lh_ref, v_ref, x_ref):
    def put(b, lo, hi, value):
        u_ref[b * NB : (b + 1) * NB, lo:hi] = value
        high, low = halves(value)
        for k, part in enumerate((high, low, high)):
            hl_ref[k * NB : (k + 1) * NB, lo:hi] = part
        if lo < K:
            e = min(hi, K)
            for k, part in enumerate((high, high, low)):
                lh_ref[k * NB : (k + 1) * NB, lo:e] = part[:, : e - lo]

    def stack(x):
        high, low = halves(x)
        return jnp.concatenate([high, low, high], axis=0)

    first_inv = K + HALF
    side_work = early
    for b in range(3):
        o, n = b * NB, (b + 1) * NB
        end = first_inv + n
        u, v = factor([a_ref[o + 8 * i : o + 8 * i + 8, o:n] for i in range(16)], side_work)
        u_ref[o:n, o:n] = u
        high, low = halves(v)
        v_ref[...] = jnp.concatenate([high, high, low], axis=1)
        put(b, n, n + NB, dot(v_ref[...], stack(a_ref[o:n, n : n + NB])))
        a_ref[n : n + NB, n : n + NB] -= dot(
            lh_ref[:, n : n + NB], hl_ref[:, n : n + NB], ((0,), (0,))
        )
        put(b, first_inv + o, end, v)

        def rest(b=b, o=o, n=n):
            lo, hi = n + NB, first_inv + o
            put(b, lo, hi, dot(v_ref[...], stack(a_ref[o:n, lo:hi])))

        def trail(r, lo, end=end):
            rows = slice(r * NB, (r + 1) * NB)
            a_ref[rows, lo:end] -= dot(lh_ref[:, rows], hl_ref[:, lo:end], ((0,), (0,)))

        def partial(o=o, n=n, end=end):
            y = u_ref[o:n, K:first_inv].astype(BF16)
            part = dot(
                hl_ref[: 2 * NB, first_inv:end], jnp.concatenate([y, y], axis=0), ((0,), (0,))
            )
            if o:
                x_ref[:o, :] += part[:o]
            x_ref[o:n, :] = part[o:]

        side_work = [rest, functools.partial(trail, b + 1, n + NB)]
        side_work += [functools.partial(trail, r, r * NB) for r in range(b + 2, 4)]
        side_work.append(partial)
    o = 3 * NB
    side_work += late
    u, v = factor([a_ref[o + 8 * i : o + 8 * i + 8, o:K] for i in range(16)], side_work)
    u_ref[o:K, o:K] = u
    high, low = halves(v)
    yw = dot(jnp.concatenate([high, high, low], axis=1), stack(a_ref[o:K, K : first_inv + o]))
    y = yw[:, :HALF].astype(BF16)
    high, low = halves(jnp.concatenate([yw[:, HALF:], v], axis=1))
    part = dot(
        jnp.concatenate([high, low], axis=0), jnp.concatenate([y, y], axis=0), ((0,), (0,))
    )
    return jnp.concatenate([x_ref[:o, :] + part[:o], part[o:]], axis=0)


def solve_body(core, pack_ref, other_ref, left_ref, count, late, right_ref, g_ref, t_ref, a_ref,
               *scratch):
    pieces = pack_ref.shape[0]
    part, step = NG // pieces, 2 * K // pieces
    where = {ij: (c, n * NB) for c in range(2) for n, ij in enumerate(BLOCKS[c])}
    diag = lax.broadcasted_iota(jnp.int32, (NB, NB), 0) == lax.broadcasted_iota(
        jnp.int32, (NB, NB), 1
    )
    ready = set()
    root, qrow, qcol = [None] * 4, [None] * 4, [None] * 4

    def unpack(c, p):
        for i in range(p // part, (p + NB - 1) // part + 1):
            if (c, i) not in ready:
                ready.add((c, i))
                mine, theirs = pack_ref[i].astype(F32), other_ref[i].astype(F32)
                t_ref[i] = jnp.where(core == c, mine, theirs)
                q = c * NG + i * part
                g_ref[q : q + part, :] = t_ref[i, :part, :]

    def block(i, j):
        c, p = where[i, j]
        unpack(c, p)
        mean = dot(
            left_ref[:pieces, i * NB : (i + 1) * NB],
            left_ref[:pieces, j * NB : (j + 1) * NB],
            ((0,), (0,)),
        )
        return g_ref[c * NG + p : c * NG + p + NB, :] + count * mean

    def diagonal(b):
        g = block(b, b)
        only = jnp.where(diag, g, 0.0)
        row = jnp.sum(only, axis=0, keepdims=True)
        qrow[b] = lax.rsqrt(row)
        qcol[b] = lax.rsqrt(jnp.sum(only, axis=1, keepdims=True))
        root[b] = row * qrow[b]
        rows = slice(b * NB, (b + 1) * NB)
        a_ref[rows, rows] = g * qcol[b] * qrow[b]

    def off_diagonal(i, j):
        a_ref[i * NB : (i + 1) * NB, j * NB : (j + 1) * NB] = block(i, j) * qcol[i] * qrow[j]

    def sums():
        for i in range(pieces):
            e = pack_ref[i].astype(F32)[part + step :]
            for k in range(2):
                for h in range(2):
                    q = pieces * k + i
                    right_ref[q : q + 1, h * NB : (h + 1) * NB] = e[2 * k + h : 2 * k + h + 1]

    def right_side(b):
        rows = slice(b * NB, (b + 1) * NB)
        mean = dot(left_ref[:, rows], right_ref[...].astype(BF16), ((0,), (0,)))
        for h in range(2):
            for o in range(b * NB, (b + 1) * NB, step):
                i = (h * K + o) // step
                lanes = slice(K + h * NB, K + (h + 1) * NB)
                c = pack_ref[i].astype(F32)[part : part + step]
                q = o - b * NB
                a_ref[o : o + step, lanes] = c + mean[q : q + step, h * NB : (h + 1) * NB]
        a_ref[rows, K : K + HALF] *= qcol[b]
        a_ref[rows, K + HALF :] = jnp.zeros((NB, K), F32)

    diagonal(0)
    early = [functools.partial(diagonal, b) for b in range(1, 4)]
    early += [functools.partial(off_diagonal, i, j) for i in range(4) for j in range(i + 1, 4)]
    early += [sums] + [functools.partial(right_side, b) for b in range(4)]
    x = solve(early, late, a_ref, *scratch)
    rows = [(x[b * NB : (b + 1) * NB] * qcol[b]).astype(BF16) for b in range(4)]
    return jnp.concatenate(rows, axis=0), root


def block_weights(w_ref, bd_ref):
    group, width = w_ref.shape[1:]
    assert group & (group - 1) == 0

    def write(tap):
        bi = lax.broadcasted_iota(jnp.int32, (width, width), 0)
        bj = lax.broadcasted_iota(jnp.int32, (width, width), 1)
        tiled = jnp.concatenate([w_ref[tap].astype(F32)] * (width // group), axis=0)
        shift = group.bit_length() - 1
        same = lax.shift_right_logical(bi, shift) == lax.shift_right_logical(bj, shift)
        at = tap * width
        rows = pl.ds(at if isinstance(tap, int) else pl.multiple_of(at, width), width)
        bd_ref[rows, :] = jnp.where(same, tiled, 0.0).astype(BF16)

    return write


def quotient(x, by, limit):
    factor = (1 << 16) // by + 1
    assert all((k * factor) >> 16 == k // by for k in range(limit))
    return lax.shift_right_logical(x * factor, 16)


def conv_body(core, p_ref, r_ref, keep_ref, send_ref, pad_ref, win_ref, bd_ref):
    n = r_ref.shape[0]
    width = r_ref.shape[1]
    row = lax.broadcasted_iota(jnp.int32, (n, NB), 0)
    q = row - SIDE * SIDE * quotient(row, SIDE * SIDE, n)
    y = quotient(q, SIDE, SIDE * SIDE)
    x = q - SIDE * y
    for tap in range(9):
        a, b = tap // 3 - 1, tap % 3 - 1
        d = 8 + a * SIDE + b
        ok = None
        if a:
            ok = (y > 0) if a < 0 else (y < SIDE - 1)
        if b:
            okx = (x > 0) if b < 0 else (x < SIDE - 1)
            ok = okx if ok is None else ok & okx
        for h in range(0, width, NB):
            window = pad_ref[d : d + n, h : h + NB]
            if ok is not None:
                window = jnp.where(ok, window, 0.0)
            win_ref[:, tap * width + h : tap * width + h + NB] = window.astype(BF16)
    r = dot(win_ref[...], bd_ref[...]).astype(BF16)
    r_ref[...] = r
    mine = pl.multiple_of(core * HALF, HALF)
    theirs = pl.multiple_of((1 - core) * HALF, HALF)
    send_ref[...] = dot(r, p_ref[:, pl.ds(theirs, HALF)]).astype(BF16)
    keep_ref[...] = dot(r, p_ref[:, pl.ds(mine, HALF)])


def pad_field(pad_ref, field):
    n, width = field.shape
    pad_ref[0:8, :] = jnp.zeros((8, width), F32)
    pad_ref[8 + n : 16 + n, :] = jnp.zeros((8, width), F32)
    pad_ref[8 : 8 + n, :] = field


def first_kernel(core_ref, f_hbm, w_hbm, p_hbm, r_ref, keep_ref, send_ref, pad_ref, win_ref, bd_ref,
                 f_ref, w_ref, p_ref, sems):
    copies = [
        pltpu.make_async_copy(src, dst, sems.at[k])
        for k, (src, dst) in enumerate(((w_hbm, w_ref), (f_hbm, f_ref), (p_hbm, p_ref)))
    ]
    for copy in copies:
        copy.start()
    copies[0].wait()
    write = block_weights(w_ref, bd_ref)
    pl.loop(0, 9)(write)
    copies[1].wait()
    pad_field(pad_ref, f_ref[...].astype(F32))
    copies[2].wait()
    conv_body(core_ref[0], p_ref, r_ref, keep_ref, send_ref, pad_ref, win_ref, bd_ref)


def middle_kernel(count, core_ref, pack_ref, other_ref, left_ref, s_ref, w_ref, p_ref,
                  r_ref, keep_ref, send_ref, pad_ref, win_ref, bd_ref, *scratch):
    core = core_ref[0]
    late = [functools.partial(block_weights(w_ref, bd_ref), tap) for tap in range(9)]
    mapped, _ = solve_body(core, pack_ref, other_ref, left_ref, count, late, *scratch)
    restored = dot(s_ref[...], mapped).astype(BF16).astype(F32)
    pad_field(pad_ref, jnp.maximum(restored, 0.0))
    conv_body(core, p_ref, r_ref, keep_ref, send_ref, pad_ref, win_ref, bd_ref)


def last_kernel(count, scale, core_ref, pack_ref, other_ref, left_ref, s_ref, out_ref, tri_ref,
                right_ref, g_ref, t_ref, a_ref, u_ref, *scratch):
    mapped, root = solve_body(
        core_ref[0], pack_ref, other_ref, left_ref, count, [], right_ref, g_ref, t_ref, a_ref,
        u_ref, *scratch,
    )
    out_ref[...] = dot(s_ref[...], mapped).astype(BF16)
    for b in range(4):
        lanes = slice(b * NB, (b + 1) * NB)
        rows = (b + 1) * NB
        tri_ref[:rows, lanes] = u_ref[:rows, lanes] * (root[b] * scale)
        if rows < K:
            tri_ref[rows:, lanes] = jnp.zeros((K - rows, NB), F32)


def gram_kernel(core_ref, own_ref, other_ref, r_ref, s_ref, m_ref, sums_ref, g_ref, t_ref):
    core = core_ref[0]
    n = own_ref.shape[0]
    pieces = t_ref.shape[0]
    s_ref[:, pl.ds(pl.multiple_of(core * HALF, HALF), HALF)] = own_ref[...]
    s_ref[:, pl.ds(pl.multiple_of((1 - core) * HALF, HALF), HALF)] = other_ref[...]
    s, r = s_ref[...], r_ref[...]
    ones = jnp.ones((8, n), BF16)
    mean = (dot(ones, s) * (1.0 / n)).astype(BF16).astype(F32)
    total = dot(ones, r)
    high = total.astype(BF16).astype(F32)
    low = (total - high).astype(BF16).astype(F32)
    first = lax.broadcasted_iota(jnp.int32, (8, K), 0) < 1
    left = jnp.where(lax.broadcasted_iota(jnp.int32, (8, K), 0) < 2, mean, 0.0).astype(BF16)
    only = jnp.where(first, mean, 0.0).astype(BF16)
    right = jnp.where(first[:, :HALF], high, low).astype(BF16)
    cross = dot(s, r, ((0,), (0,))) - dot(left, right, ((0,), (0,)))
    extra = jnp.concatenate([mean[:1, h * NB : (h + 1) * NB] for h in range(4)], axis=0)
    sums = [x[:1, h * NB : (h + 1) * NB] for x in (high, low) for h in range(2)]
    sums_ref[...] = jnp.concatenate(sums + sums, axis=0)
    for c in range(2):

        @pl.when(core == c)
        def _():
            for k, (i, j) in enumerate(BLOCKS[c]):
                a, b = slice(i * NB, (i + 1) * NB), slice(j * NB, (j + 1) * NB)
                block = dot(s_ref[:, a], s_ref[:, b], ((0,), (0,)))
                g_ref[k * NB : (k + 1) * NB, :] = block - n * dot(
                    only[:, a], only[:, b], ((0,), (0,))
                )

    part = NG // pieces
    step = 2 * K // pieces
    for i in range(pieces):
        t_ref[i, :part, :] = g_ref[i * part : (i + 1) * part, :]
        h, o = divmod(i * step, K)
        t_ref[i, part : part + step, :] = cross[o : o + step, h * NB : (h + 1) * NB]
        t_ref[i, part + step :, :] = extra
    m_ref[...] = t_ref[...].astype(BF16)


def sum_kernel(core_ref, parts_ref, sums_ref, out_ref, left_ref, l_ref):
    pieces = parts_ref.shape[0]
    used = (NG + 2 * K) // pieces
    acc = None
    for i in range(pieces):
        piece = parts_ref[i].astype(F32)
        acc = piece if acc is None else acc + piece
        for h in range(4):
            mean = piece[used + h : used + h + 1]
            for k in range(2):
                q = pieces * k + i
                l_ref[q : q + 1, h * NB : (h + 1) * NB] = mean
    total = jnp.concatenate([acc[:used], sums_ref[: PIECE - used, :]], axis=0).astype(BF16)
    for i in range(pieces):
        out_ref[i] = total
    left_ref[...] = l_ref[...].astype(BF16)


def fold_kernel(core_ref, parts_ref, out_ref):
    acc = parts_ref[0].astype(F32)
    for i in range(1, parts_ref.shape[0]):
        acc = acc + parts_ref[i].astype(F32)
    out_ref[...] = acc.astype(BF16)


def solve_scratch(pieces):
    total = 2 * K + HALF
    return [
        pltpu.VMEM((2 * pieces, HALF), F32),
        pltpu.VMEM((2 * NG, NB), F32),
        pltpu.VMEM((pieces, PIECE, NB), F32),
        pltpu.VMEM((K, total), F32),
        pltpu.VMEM((K, total), F32),
        pltpu.VMEM((3 * NB, total), BF16),
        pltpu.VMEM((3 * NB, K), BF16),
        pltpu.VMEM((NB, 3 * NB), BF16),
        pltpu.VMEM((K, HALF), F32),
    ]


def conv_scratch(n, width):
    return [
        pltpu.VMEM((n + 16, width), F32),
        pltpu.VMEM((n, 9 * width), BF16),
        pltpu.VMEM((9 * width, width), BF16),
    ]


def conv_outs(n, width):
    return (
        jax.ShapeDtypeStruct((n, width), BF16),
        jax.ShapeDtypeStruct((n, HALF), F32),
        jax.ShapeDtypeStruct((n, HALF), BF16),
    )


def call(kernel, name, outs, args, scratch=(), space=VMEM):
    return pl.pallas_call(
        kernel,
        out_shape=outs,
        in_specs=[SMEM] + [space] * (len(args) - 1),
        out_specs=jax.tree.map(lambda _: VMEM, outs),
        scratch_shapes=list(scratch),
        compiler_params=PARAMS,
        name=name,
    )(*args)


SWAP = ((0, 1), (1, 0))
ROWS = ("y", "z")


def spread(x, axes):
    n = lax.axis_size(axes)
    return lax.all_to_all(jnp.broadcast_to(x[None], (n,) + x.shape), axes, 0, 0)


def sketch_of(core, keep, send):
    pair = (keep + lax.ppermute(send, "core", SWAP).astype(F32)).astype(BF16)
    own = call(
        fold_kernel, "fold", jax.ShapeDtypeStruct(pair.shape, BF16), (core, spread(pair, "x"))
    )
    return own, lax.ppermute(own, "core", SWAP)


def compress_sums(core, r, keep, send):
    own, other = sketch_of(core, keep, send)
    n = r.shape[0]
    pieces = lax.axis_size(ROWS)
    outs = (
        jax.ShapeDtypeStruct((n, K), BF16),
        jax.ShapeDtypeStruct((pieces, PIECE, NB), BF16),
        jax.ShapeDtypeStruct((8, NB), F32),
    )
    scratch = [pltpu.VMEM((NG, NB), F32), pltpu.VMEM((pieces, PIECE, NB), F32)]
    s, m, sums = call(gram_kernel, "gram", outs, (core, own, other, r), scratch)
    parts = lax.all_to_all(m, ROWS, 0, 0)
    outs = (
        jax.ShapeDtypeStruct((pieces, PIECE, NB), BF16),
        jax.ShapeDtypeStruct((2 * pieces, K), BF16),
    )
    scratch = [pltpu.VMEM((2 * pieces, K), F32)]
    total, left = call(sum_kernel, "sum", outs, (core, parts, sums), scratch)
    pack = lax.all_to_all(total, ROWS, 0, 0)
    return pack, lax.ppermute(pack, "core", SWAP), left, s


def per_device(inputs, conv_one, conv_two, probe_one, probe_two):
    n, width = inputs.shape
    pieces = lax.axis_size(ROWS)
    total_rows = n * pieces
    core = lax.axis_index("core").astype(jnp.int32).reshape(1)
    outs = conv_outs(n, width)
    args = (inputs, conv_one, probe_one)
    scratch = conv_scratch(n, width) + [pltpu.VMEM(x.shape, x.dtype) for x in args]
    scratch.append(pltpu.SemaphoreType.DMA((len(args),)))
    pinned = [pltpu.with_memory_space_constraint(x, pltpu.HBM) for x in args]
    r, keep, send = call(first_kernel, "first", outs, (core, *pinned), scratch, HBM)
    sums = compress_sums(core, r, keep, send)
    r, keep, send = call(
        functools.partial(middle_kernel, n), "middle", outs, (core, *sums, conv_two, probe_two),
        conv_scratch(n, width) + solve_scratch(pieces),
    )
    sums = compress_sums(core, r, keep, send)
    outs = (jax.ShapeDtypeStruct((n, width), BF16), jax.ShapeDtypeStruct((K, K), F32))
    return call(
        functools.partial(last_kernel, n, 1.0 / math.sqrt(total_rows)), "last", outs, (core, *sums),
        solve_scratch(pieces),
    )


def solution(mesh):
    grid = Mesh(mesh.devices.reshape(8, 4, 4, 2), ("z", "y", "x", "core"))
    rows, chan = ("z", "y"), ("x", "core")
    in_specs = (
        P(rows, chan),
        P(None, None, chan),
        P(None, None, chan),
        P(chan, None),
        P(chan, None),
    )
    out_specs = (P(rows, chan), P())
    return jax.shard_map(
        per_device, mesh=grid, in_specs=in_specs, out_specs=out_specs, check_vma=False
    )
```

```python
import functools
import math

import jax
import jax.numpy as jnp
from jax import lax
from jax.experimental import pallas as pl
from jax.experimental.pallas import tpu as pltpu
from jax.sharding import Mesh, PartitionSpec as P

SIDE = 7
K = 512
NB = 128
HALF = 256
F32 = jnp.float32
BF16 = jnp.bfloat16
VMEM = pl.BlockSpec(memory_space=pltpu.VMEM)
SMEM = pl.BlockSpec(memory_space=pltpu.SMEM)
HBM = pl.BlockSpec(memory_space=pltpu.HBM)
PARAMS = pltpu.CompilerParams(vmem_limit_bytes=48 << 20)
BLOCKS = (((0, 0), (0, 1), (0, 2), (0, 3), (1, 1)), ((1, 2), (1, 3), (2, 2), (2, 3), (3, 3)))
NG = 5 * NB
PIECE = 56


def dot(a, b, dims=((1,), (0,))):
    return lax.dot_general(a, b, (dims, ((), ())), preferred_element_type=F32)


def bcast_lane(x, k):
    return jnp.broadcast_to(x[:, k : k + 1], (8, NB))


def bcast_row(x, k):
    return jnp.broadcast_to(x[k : k + 1, :], (8, NB))


def combine(coeffs, rows):
    p = [c * b for c, b in zip(coeffs, rows)]
    while len(p) > 1:
        p = [p[i] + p[i + 1] for i in range(0, len(p), 2)]
    return p[0]


def halves(x):
    high = x.astype(BF16)
    return high, (x - high.astype(F32)).astype(BF16)


def factor(rows, side_work):
    n = len(rows)
    sub = lax.broadcasted_iota(jnp.int32, (8, NB), 0)
    lane = lax.broadcasted_iota(jnp.int32, (8, NB), 1)
    at = [sub == i for i in range(8)]
    zero = jnp.zeros((8, NB), F32)
    unit = [(sub == i).astype(F32) for i in range(8)]
    inv = [(lane == sub + 8 * r).astype(F32) for r in range(n)]
    rows, side_work = list(rows), list(side_work)
    upper, lower_inv = [], []
    for r in range(n):
        top, top_inv = rows[r], inv[r]
        cols = [bcast_lane(top, 8 * r + k) for k in range(8)]
        rb = [bcast_row(top, j) for j in range(8)]
        ib = [bcast_row(top_inv, j) for j in range(8)]
        pivots = []
        for p in range(0, 8, 2):
            a, b, c = bcast_row(cols[p], p), bcast_row(cols[p], p + 1), bcast_row(cols[p + 1], p + 1)
            det = a * c - b * b
            idet = 1.0 / det
            w0 = cols[p] * c - cols[p + 1] * b
            w1 = cols[p + 1] * a - cols[p] * b
            w0 = jnp.where(at[p], det - c, jnp.where(at[p + 1], b, w0))
            w1 = jnp.where(at[p], b, jnp.where(at[p + 1], det - a, w1))
            z0, z1 = w0 * idet, w1 * idet
            new, above = list(cols), {}
            for j in range(8):
                if j in (p, p + 1):
                    continue
                s0, s1 = bcast_row(cols[j], p), bcast_row(cols[j], p + 1)
                if j in (p + 2, p + 3):
                    new[j] = cols[j] - (w0 * s0 + w1 * s1) * idet
                else:
                    new[j] = cols[j] - (z0 * s0 + z1 * s1)
                if j > p:
                    above[j] = (s0, s1)
            new[p], new[p + 1] = unit[p] - z0, unit[p + 1] - z1
            pivots.append((p, a, b, det, above))
            cols = new
        x, xi = combine(cols, rb), combine(cols, ib)
        xb = [bcast_row(x, k) for k in range(8)]
        xib = [bcast_row(xi, k) for k in range(8)]
        for g in range(r + 1, n):
            cg = [bcast_lane(rows[g], 8 * r + k) for k in range(8)]
            rows[g], inv[g] = rows[g] - combine(cg, xb), inv[g] - combine(cg, xib)
        ldl, d = [zero] * 8, zero
        for p, a, b, det, above in pivots:
            ia = 1.0 / a
            ratio, second = b * ia, det * ia
            d = jnp.where(at[p], a, jnp.where(at[p + 1], second, d))
            ldl[p] = jnp.where(at[p], a, ldl[p])
            ldl[p + 1] = jnp.where(at[p], b, jnp.where(at[p + 1], second, ldl[p + 1]))
            for j, (s0, s1) in above.items():
                ldl[j] = jnp.where(at[p], s0, jnp.where(at[p + 1], s1 - ratio * s0, ldl[j]))
        q = lax.rsqrt(d)
        upper.append(jnp.where(lane >= 8 * r + sub, q * combine(ldl, xb), 0.0))
        lower_inv.append(q * combine(ldl, xib))
        if r < n - 1:
            k = -(-len(side_work) // (n - 1 - r))
            for work in side_work[:k]:
                work()
            side_work = side_work[k:]
    return jnp.concatenate(upper, axis=0), jnp.concatenate(lower_inv, axis=0)


def solve(early, late, a_ref, u_ref, hl_ref, lh_ref, v_ref, x_ref):
    def put(b, lo, hi, value):
        u_ref[b * NB : (b + 1) * NB, lo:hi] = value
        high, low = halves(value)
        for k, part in enumerate((high, low, high)):
            hl_ref[k * NB : (k + 1) * NB, lo:hi] = part
        if lo < K:
            e = min(hi, K)
            for k, part in enumerate((high, high, low)):
                lh_ref[k * NB : (k + 1) * NB, lo:e] = part[:, : e - lo]

    def stack(x):
        high, low = halves(x)
        return jnp.concatenate([high, low, high], axis=0)

    first_inv = K + HALF
    side_work = early
    for b in range(3):
        o, n = b * NB, (b + 1) * NB
        end = first_inv + n
        u, v = factor([a_ref[o + 8 * i : o + 8 * i + 8, o:n] for i in range(16)], side_work)
        u_ref[o:n, o:n] = u
        high, low = halves(v)
        v_ref[...] = jnp.concatenate([high, high, low], axis=1)
        put(b, n, n + NB, dot(v_ref[...], stack(a_ref[o:n, n : n + NB])))
        a_ref[n : n + NB, n : n + NB] -= dot(
            lh_ref[:, n : n + NB], hl_ref[:, n : n + NB], ((0,), (0,))
        )
        put(b, first_inv + o, end, v)

        def rest(b=b, o=o, n=n):
            lo, hi = n + NB, first_inv + o
            put(b, lo, hi, dot(v_ref[...], stack(a_ref[o:n, lo:hi])))

        def trail(r, lo, end=end):
            rows = slice(r * NB, (r + 1) * NB)
            a_ref[rows, lo:end] -= dot(lh_ref[:, rows], hl_ref[:, lo:end], ((0,), (0,)))

        def partial(o=o, n=n, end=end):
            y = u_ref[o:n, K:first_inv].astype(BF16)
            part = dot(
                hl_ref[: 2 * NB, first_inv:end], jnp.concatenate([y, y], axis=0), ((0,), (0,))
            )
            if o:
                x_ref[:o, :] += part[:o]
            x_ref[o:n, :] = part[o:]

        side_work = [rest, functools.partial(trail, b + 1, n + NB)]
        side_work += [functools.partial(trail, r, r * NB) for r in range(b + 2, 4)]
        side_work.append(partial)
    o = 3 * NB
    side_work += late
    u, v = factor([a_ref[o + 8 * i : o + 8 * i + 8, o:K] for i in range(16)], side_work)
    u_ref[o:K, o:K] = u
    high, low = halves(v)
    yw = dot(jnp.concatenate([high, high, low], axis=1), stack(a_ref[o:K, K : first_inv + o]))
    y = yw[:, :HALF].astype(BF16)
    high, low = halves(jnp.concatenate([yw[:, HALF:], v], axis=1))
    part = dot(
        jnp.concatenate([high, low], axis=0), jnp.concatenate([y, y], axis=0), ((0,), (0,))
    )
    return jnp.concatenate([x_ref[:o, :] + part[:o], part[o:]], axis=0)


def solve_body(core, pack_ref, other_ref, left_ref, count, late, right_ref, g_ref, t_ref, a_ref,
               *scratch):
    pieces = pack_ref.shape[0]
    part, step = NG // pieces, 2 * K // pieces
    where = {ij: (c, n * NB) for c in range(2) for n, ij in enumerate(BLOCKS[c])}
    diag = lax.broadcasted_iota(jnp.int32, (NB, NB), 0) == lax.broadcasted_iota(
        jnp.int32, (NB, NB), 1
    )
    ready = set()
    root, qrow, qcol = [None] * 4, [None] * 4, [None] * 4

    def unpack(c, p):
        for i in range(p // part, (p + NB - 1) // part + 1):
            if (c, i) not in ready:
                ready.add((c, i))
                mine, theirs = pack_ref[i].astype(F32), other_ref[i].astype(F32)
                t_ref[i] = jnp.where(core == c, mine, theirs)
                q = c * NG + i * part
                g_ref[q : q + part, :] = t_ref[i, :part, :]

    def block(i, j):
        c, p = where[i, j]
        unpack(c, p)
        mean = dot(
            left_ref[:pieces, i * NB : (i + 1) * NB],
            left_ref[:pieces, j * NB : (j + 1) * NB],
            ((0,), (0,)),
        )
        return g_ref[c * NG + p : c * NG + p + NB, :] + count * mean

    def diagonal(b):
        g = block(b, b)
        only = jnp.where(diag, g, 0.0)
        row = jnp.sum(only, axis=0, keepdims=True)
        qrow[b] = lax.rsqrt(row)
        qcol[b] = lax.rsqrt(jnp.sum(only, axis=1, keepdims=True))
        root[b] = row * qrow[b]
        rows = slice(b * NB, (b + 1) * NB)
        a_ref[rows, rows] = g * qcol[b] * qrow[b]

    def off_diagonal(i, j):
        a_ref[i * NB : (i + 1) * NB, j * NB : (j + 1) * NB] = block(i, j) * qcol[i] * qrow[j]

    def sums():
        for i in range(pieces):
            e = pack_ref[i].astype(F32)[part + step :]
            for k in range(2):
                for h in range(2):
                    q = pieces * k + i
                    right_ref[q : q + 1, h * NB : (h + 1) * NB] = e[2 * k + h : 2 * k + h + 1]

    def right_side(b):
        rows = slice(b * NB, (b + 1) * NB)
        mean = dot(left_ref[:, rows], right_ref[...].astype(BF16), ((0,), (0,)))
        for h in range(2):
            for o in range(b * NB, (b + 1) * NB, step):
                i = (h * K + o) // step
                lanes = slice(K + h * NB, K + (h + 1) * NB)
                c = pack_ref[i].astype(F32)[part : part + step]
                q = o - b * NB
                a_ref[o : o + step, lanes] = c + mean[q : q + step, h * NB : (h + 1) * NB]
        a_ref[rows, K : K + HALF] *= qcol[b]
        a_ref[rows, K + HALF :] = jnp.zeros((NB, K), F32)

    diagonal(0)
    early = [functools.partial(diagonal, b) for b in range(1, 4)]
    early += [functools.partial(off_diagonal, i, j) for i in range(4) for j in range(i + 1, 4)]
    early += [sums] + [functools.partial(right_side, b) for b in range(4)]
    x = solve(early, late, a_ref, *scratch)
    rows = [(x[b * NB : (b + 1) * NB] * qcol[b]).astype(BF16) for b in range(4)]
    return jnp.concatenate(rows, axis=0), root


def block_weights(w_ref, bd_ref):
    group, width = w_ref.shape[1:]
    assert group & (group - 1) == 0

    def write(tap):
        bi = lax.broadcasted_iota(jnp.int32, (width, width), 0)
        bj = lax.broadcasted_iota(jnp.int32, (width, width), 1)
        tiled = jnp.concatenate([w_ref[tap].astype(F32)] * (width // group), axis=0)
        shift = group.bit_length() - 1
        same = lax.shift_right_logical(bi, shift) == lax.shift_right_logical(bj, shift)
        at = tap * width
        rows = pl.ds(at if isinstance(tap, int) else pl.multiple_of(at, width), width)
        bd_ref[rows, :] = jnp.where(same, tiled, 0.0).astype(BF16)

    return write


def quotient(x, by, limit):
    factor = (1 << 16) // by + 1
    assert all((k * factor) >> 16 == k // by for k in range(limit))
    return lax.shift_right_logical(x * factor, 16)


def conv_body(core, p_ref, r_ref, keep_ref, send_ref, pad_ref, win_ref, bd_ref):
    n = r_ref.shape[0]
    width = r_ref.shape[1]
    row = lax.broadcasted_iota(jnp.int32, (n, NB), 0)
    q = row - SIDE * SIDE * quotient(row, SIDE * SIDE, n)
    y = quotient(q, SIDE, SIDE * SIDE)
    x = q - SIDE * y
    for tap in range(9):
        a, b = tap // 3 - 1, tap % 3 - 1
        d = 8 + a * SIDE + b
        ok = None
        if a:
            ok = (y > 0) if a < 0 else (y < SIDE - 1)
        if b:
            okx = (x > 0) if b < 0 else (x < SIDE - 1)
            ok = okx if ok is None else ok & okx
        for h in range(0, width, NB):
            window = pad_ref[d : d + n, h : h + NB]
            if ok is not None:
                window = jnp.where(ok, window, 0.0)
            win_ref[:, tap * width + h : tap * width + h + NB] = window.astype(BF16)
    r = dot(win_ref[...], bd_ref[...]).astype(BF16)
    r_ref[...] = r
    mine = pl.multiple_of(core * HALF, HALF)
    theirs = pl.multiple_of((1 - core) * HALF, HALF)
    send = dot(r, p_ref[:, pl.ds(theirs, HALF)]).astype(BF16)
    keep = dot(r, p_ref[:, pl.ds(mine, HALF)])
    for h in range(2):
        send_ref[h] = send[:, h * NB : (h + 1) * NB]
        keep_ref[h] = keep[:, h * NB : (h + 1) * NB]


def pad_field(pad_ref, field):
    n, width = field.shape
    pad_ref[0:8, :] = jnp.zeros((8, width), F32)
    pad_ref[8 + n : 16 + n, :] = jnp.zeros((8, width), F32)
    pad_ref[8 : 8 + n, :] = field


def first_kernel(core_ref, f_hbm, w_hbm, p_hbm, r_ref, keep_ref, send_ref, pad_ref, win_ref, bd_ref,
                 f_ref, w_ref, p_ref, sems):
    copies = [
        pltpu.make_async_copy(src, dst, sems.at[k])
        for k, (src, dst) in enumerate(((w_hbm, w_ref), (f_hbm, f_ref), (p_hbm, p_ref)))
    ]
    for copy in copies:
        copy.start()
    copies[0].wait()
    write = block_weights(w_ref, bd_ref)
    pl.loop(0, 9)(write)
    copies[1].wait()
    pad_field(pad_ref, f_ref[...].astype(F32))
    copies[2].wait()
    conv_body(core_ref[0], p_ref, r_ref, keep_ref, send_ref, pad_ref, win_ref, bd_ref)


def middle_kernel(count, core_ref, pack_ref, other_ref, left_ref, s_ref, w_ref, p_ref,
                  r_ref, keep_ref, send_ref, pad_ref, win_ref, bd_ref, *scratch):
    core = core_ref[0]
    late = [functools.partial(block_weights(w_ref, bd_ref), tap) for tap in range(9)]
    mapped, _ = solve_body(core, pack_ref, other_ref, left_ref, count, late, *scratch)
    restored = dot(s_ref[...], mapped).astype(BF16).astype(F32)
    pad_field(pad_ref, jnp.maximum(restored, 0.0))
    conv_body(core, p_ref, r_ref, keep_ref, send_ref, pad_ref, win_ref, bd_ref)


def last_kernel(count, scale, core_ref, pack_ref, other_ref, left_ref, s_ref, out_ref, tri_ref,
                right_ref, g_ref, t_ref, a_ref, u_ref, *scratch):
    mapped, root = solve_body(
        core_ref[0], pack_ref, other_ref, left_ref, count, [], right_ref, g_ref, t_ref, a_ref,
        u_ref, *scratch,
    )
    out_ref[...] = dot(s_ref[...], mapped).astype(BF16)
    for b in range(4):
        lanes = slice(b * NB, (b + 1) * NB)
        rows = (b + 1) * NB
        tri_ref[:rows, lanes] = u_ref[:rows, lanes] * (root[b] * scale)
        if rows < K:
            tri_ref[rows:, lanes] = jnp.zeros((K - rows, NB), F32)


def gram_kernel(core_ref, own_ref, other_ref, r_ref, s_ref, m_ref, sums_ref, g_ref, t_ref):
    core = core_ref[0]
    n = own_ref.shape[1]
    pieces = t_ref.shape[0]
    for h in range(2):
        s_ref[:, pl.ds(pl.multiple_of(core * HALF + h * NB, NB), NB)] = own_ref[h]
        s_ref[:, pl.ds(pl.multiple_of((1 - core) * HALF + h * NB, NB), NB)] = other_ref[h]
    s, r = s_ref[...], r_ref[...]
    ones = jnp.ones((8, n), BF16)
    mean = (dot(ones, s) * (1.0 / n)).astype(BF16).astype(F32)
    total = dot(ones, r)
    high = total.astype(BF16).astype(F32)
    low = (total - high).astype(BF16).astype(F32)
    first = lax.broadcasted_iota(jnp.int32, (8, K), 0) < 1
    left = jnp.where(lax.broadcasted_iota(jnp.int32, (8, K), 0) < 2, mean, 0.0).astype(BF16)
    only = jnp.where(first, mean, 0.0).astype(BF16)
    right = jnp.where(first[:, :HALF], high, low).astype(BF16)
    cross = dot(s, r, ((0,), (0,))) - dot(left, right, ((0,), (0,)))
    extra = jnp.concatenate([mean[:1, h * NB : (h + 1) * NB] for h in range(4)], axis=0)
    sums = [x[:1, h * NB : (h + 1) * NB] for x in (high, low) for h in range(2)]
    sums_ref[...] = jnp.concatenate(sums + sums, axis=0)
    for c in range(2):

        @pl.when(core == c)
        def _():
            for k, (i, j) in enumerate(BLOCKS[c]):
                a, b = slice(i * NB, (i + 1) * NB), slice(j * NB, (j + 1) * NB)
                block = dot(s_ref[:, a], s_ref[:, b], ((0,), (0,)))
                g_ref[k * NB : (k + 1) * NB, :] = block - n * dot(
                    only[:, a], only[:, b], ((0,), (0,))
                )

    part = NG // pieces
    step = 2 * K // pieces
    for i in range(pieces):
        t_ref[i, :part, :] = g_ref[i * part : (i + 1) * part, :]
        h, o = divmod(i * step, K)
        t_ref[i, part : part + step, :] = cross[o : o + step, h * NB : (h + 1) * NB]
        t_ref[i, part + step :, :] = extra
    m_ref[...] = t_ref[...].astype(BF16)


def sum_kernel(core_ref, parts_ref, sums_ref, out_ref, left_ref, l_ref):
    pieces = parts_ref.shape[0]
    used = (NG + 2 * K) // pieces
    acc = None
    for i in range(pieces):
        piece = parts_ref[i].astype(F32)
        acc = piece if acc is None else acc + piece
        for h in range(4):
            mean = piece[used + h : used + h + 1]
            for k in range(2):
                q = pieces * k + i
                l_ref[q : q + 1, h * NB : (h + 1) * NB] = mean
    total = jnp.concatenate([acc[:used], sums_ref[: PIECE - used, :]], axis=0).astype(BF16)
    for i in range(pieces):
        out_ref[i] = total
    left_ref[...] = l_ref[...].astype(BF16)


def fold_kernel(core_ref, parts_ref, out_ref):
    acc = parts_ref[0].astype(F32)
    for i in range(1, parts_ref.shape[0]):
        acc = acc + parts_ref[i].astype(F32)
    out_ref[...] = acc.astype(BF16)


def solve_scratch(pieces):
    total = 2 * K + HALF
    return [
        pltpu.VMEM((2 * pieces, HALF), F32),
        pltpu.VMEM((2 * NG, NB), F32),
        pltpu.VMEM((pieces, PIECE, NB), F32),
        pltpu.VMEM((K, total), F32),
        pltpu.VMEM((K, total), F32),
        pltpu.VMEM((3 * NB, total), BF16),
        pltpu.VMEM((3 * NB, K), BF16),
        pltpu.VMEM((NB, 3 * NB), BF16),
        pltpu.VMEM((K, HALF), F32),
    ]


def conv_scratch(n, width):
    return [
        pltpu.VMEM((n + 16, width), F32),
        pltpu.VMEM((n, 9 * width), BF16),
        pltpu.VMEM((9 * width, width), BF16),
    ]


def conv_outs(n, width):
    return (
        jax.ShapeDtypeStruct((n, width), BF16),
        jax.ShapeDtypeStruct((2, n, NB), F32),
        jax.ShapeDtypeStruct((2, n, NB), BF16),
    )


def call(kernel, name, outs, args, scratch=(), space=VMEM):
    return pl.pallas_call(
        kernel,
        out_shape=outs,
        in_specs=[SMEM] + [space] * (len(args) - 1),
        out_specs=jax.tree.map(lambda _: VMEM, outs),
        scratch_shapes=list(scratch),
        compiler_params=PARAMS,
        name=name,
    )(*args)


SWAP = ((0, 1), (1, 0))
ROWS = ("z", "y")


def spread(x, axes):
    n = lax.axis_size(axes)
    return lax.all_to_all(jnp.broadcast_to(x[None], (n,) + x.shape), axes, 0, 0)


def sketch_of(core, keep, send):
    pair = (keep + lax.ppermute(send, "core", SWAP).astype(F32)).astype(BF16)
    own = call(
        fold_kernel, "fold", jax.ShapeDtypeStruct(pair.shape, BF16), (core, spread(pair, "x"))
    )
    return own, lax.ppermute(own, "core", SWAP)


def compress_sums(core, r, keep, send):
    own, other = sketch_of(core, keep, send)
    n = r.shape[0]
    pieces = lax.axis_size(ROWS)
    outs = (
        jax.ShapeDtypeStruct((n, K), BF16),
        jax.ShapeDtypeStruct((pieces, PIECE, NB), BF16),
        jax.ShapeDtypeStruct((8, NB), F32),
    )
    scratch = [pltpu.VMEM((NG, NB), F32), pltpu.VMEM((pieces, PIECE, NB), F32)]
    s, m, sums = call(gram_kernel, "gram", outs, (core, own, other, r), scratch)
    parts = lax.all_to_all(m, ROWS, 0, 0)
    outs = (
        jax.ShapeDtypeStruct((pieces, PIECE, NB), BF16),
        jax.ShapeDtypeStruct((2 * pieces, K), BF16),
    )
    scratch = [pltpu.VMEM((2 * pieces, K), F32)]
    total, left = call(sum_kernel, "sum", outs, (core, parts, sums), scratch)
    pack = lax.all_to_all(total, ROWS, 0, 0)
    return pack, lax.ppermute(pack, "core", SWAP), left, s


def per_device(inputs, conv_one, conv_two, probe_one, probe_two):
    n, width = inputs.shape
    pieces = lax.axis_size(ROWS)
    total_rows = n * pieces
    core = lax.axis_index("core").astype(jnp.int32).reshape(1)
    outs = conv_outs(n, width)
    args = (inputs, conv_one, probe_one)
    scratch = conv_scratch(n, width) + [pltpu.VMEM(x.shape, x.dtype) for x in args]
    scratch.append(pltpu.SemaphoreType.DMA((len(args),)))
    pinned = [pltpu.with_memory_space_constraint(x, pltpu.HBM) for x in args]
    r, keep, send = call(first_kernel, "first", outs, (core, *pinned), scratch, HBM)
    sums = compress_sums(core, r, keep, send)
    r, keep, send = call(
        functools.partial(middle_kernel, n), "middle", outs, (core, *sums, conv_two, probe_two),
        conv_scratch(n, width) + solve_scratch(pieces),
    )
    sums = compress_sums(core, r, keep, send)
    outs = (jax.ShapeDtypeStruct((n, width), BF16), jax.ShapeDtypeStruct((K, K), F32))
    return call(
        functools.partial(last_kernel, n, 1.0 / math.sqrt(total_rows)), "last", outs, (core, *sums),
        solve_scratch(pieces),
    )


def solution(mesh):
    grid = Mesh(mesh.devices.reshape(8, 4, 4, 2), ("z", "y", "x", "core"))
    rows, chan = ("z", "y"), ("x", "core")
    in_specs = (
        P(rows, chan),
        P(None, None, chan),
        P(None, None, chan),
        P(chan, None),
        P(chan, None),
    )
    out_specs = (P(rows, chan), P())
    return jax.shard_map(
        per_device, mesh=grid, in_specs=in_specs, out_specs=out_specs, check_vma=False
    )
```
